512 devices in a mesh: dp: 32 (over z, x_lo, core), seq: 16 (over y, x_hi).
Axes of the slice: x: 4 (x_hi: 2, x_lo: 2; x = x_hi * 2 + x_lo), y: 8, z: 8, core: 2. Of those that a mesh axis runs over, the one named last changes fastest.
Arguments:
- query_in: bfloat16 [32, 2048, 2048], P('dp', 'seq'), may hold values from -6 to 6
- key_in: bfloat16 [32, 2048, 2048], P('dp', 'seq'), may hold values from -6 to 6
- value_in: bfloat16 [32, 2048, 2048], P('dp', 'seq'), may hold values from -6 to 6
- grad_out: bfloat16 [32, 2048, 2048], P('dp', 'seq'), may hold values from -6 to 6
- w_query: bfloat16 [2048, 128], replicated, may hold values from -0.5 to 0.5
- w_key: bfloat16 [2048, 128], replicated, may hold values from -0.5 to 0.5
- norm_gain: float32 [2048], replicated, may hold values from 0.1 to 1.9
Outputs:
- grad_query: bfloat16 [32, 2048, 2048], P('dp', 'seq')
- grad_key: bfloat16 [32, 2048, 2048], P('dp', 'seq')
- grad_value: bfloat16 [32, 2048, 2048], P('dp', 'seq')
- grad_w_query: float32 [2048, 128], P('dp')
- grad_w_key: float32 [2048, 128], P('dp')
- grad_gain: float32 [2048], P('dp')
The draws below stay inside these ranges and needn't reach their ends.
All inputs are finite; a program needn't handle non-finite values.
Results may differ from the reference program's by a relative error of at most 0.0077.
Values sent between devices are 32-bit elements; how exact they have to be, the bound alone decides.
A program may use at most 128 MiB of HBM per device.

```python
import jax
import jax.numpy as jnp
from jax import lax

HEAD = 128
TOK_DEV = 128
HD = 2048
LEN = 2048
BATCH = 32


def raised(values, own_key, source, target, shards_of, factor):
    def block_of(position):
        return (jnp.arange(values.shape[position]) // (values.shape[position] // shards_of)).reshape((-1,) + (1,) * (values.ndim - 1 - position))

    first = jax.random.permutation(own_key, shards_of)[block_of(target)]
    far = (block_of(target) + shards_of // 2) % shards_of
    return jnp.where((block_of(source) == first) | (block_of(source) == far), factor * values, values)


def steps_of(rng, dims, cuts, low, top_value):
    def one(position, parts):
        draws = jax.random.uniform(jax.random.fold_in(jax.random.fold_in(rng, 6), position), (parts,), jnp.float32, low / len(cuts), top_value / len(cuts))
        return jnp.repeat(jnp.exp(draws), dims[position] // parts).reshape((-1,) + (1,) * (len(dims) - position - 1))

    gain = one(*cuts[0])
    for cut in cuts[1:]:
        gain = gain * one(*cut)
    return gain


def normal_values(key, extent, deviation, limit, split=(), kind=jnp.bfloat16):
    drawn = deviation * jax.random.normal(key, extent, jnp.float32)
    if split:
        drawn = drawn * steps_of(key, extent, split, -0.22, 0.18)
    return jnp.clip(drawn, -limit, limit).astype(kind)


def bell_draw_with(stream_key, shape, scale, limit, split, heavy, kind=jnp.bfloat16):
    array = scale * jax.random.normal(stream_key, shape, jnp.float32)
    if split:
        array = array * steps_of(stream_key, shape, split, -0.22, 0.18)
    return jnp.clip(raised(array, jax.random.fold_in(stream_key, 3), *heavy), -limit, limit).astype(kind)


def setup_inputs(seed: int = 0) -> dict:
    streams_of = jax.random.split(jax.random.key(seed), 8)
    return {
        "query_in": bell_draw_with(streams_of[0], (BATCH, LEN, HD), 1.0, 6.0, ((0, 32), (1, 16)), (0, 2, 32, 2.75)),
        "key_in": bell_draw_with(streams_of[1], (BATCH, LEN, HD), 1.0, 6.0, ((0, 32), (1, 16)), (0, 2, 32, 2.75)),
        "value_in": normal_values(streams_of[2], (BATCH, LEN, HD), 1.0, 6.0, ((0, 32), (1, 16))),
        "grad_out": bell_draw_with(streams_of[3], (BATCH, LEN, HD), 1.0, 6.0, ((0, 32), (1, 16)), (0, 2, 32, 2.75)),
        "w_query": normal_values(streams_of[4], (HD, HEAD), HEAD ** -0.5, 0.5),
        "w_key": normal_values(streams_of[5], (HD, HEAD), HEAD ** -0.5, 0.5),
        "norm_gain": jnp.clip(1.0 + 0.18 * jax.random.normal(streams_of[6], (HD,), jnp.float32), 0.1, 1.9),
    }


norm_eps = 1e-05
highest = lax.Precision.HIGHEST

def rounded(tensor):
    return lax.optimization_barrier(tensor.astype(jnp.bfloat16)).astype(jnp.float32)

def one_sequence(query_in, key_in, value_in, grad_out, w_query, w_key, norm_gain):
    length, width_all = query_in.shape
    blocks = length // TOK_DEV
    head_count = width_all // HEAD

    def split_heads(tensor):
        return tensor.reshape(blocks, TOK_DEV, head_count, HEAD).astype(jnp.float32)
    query_h = split_heads(query_in)
    key_h = split_heads(key_in)
    value_h = split_heads(value_in)
    grad_f = split_heads(grad_out)
    map_query = w_query.reshape(head_count, HEAD, HEAD).astype(jnp.float32)
    map_key = w_key.reshape(head_count, HEAD, HEAD).astype(jnp.float32)
    pre_query = jnp.einsum('nthd,hde->nthe', query_h, map_query, precision=highest)
    pre_key = jnp.einsum('nthd,hde->nthe', key_h, map_key, precision=highest)
    feat_query = rounded(jax.nn.elu(pre_query) + 1.0)
    feat_key = rounded(jax.nn.elu(pre_key) + 1.0)
    causal = jnp.tril(jnp.ones((TOK_DEV, TOK_DEV), dtype=bool))
    local_state = jnp.einsum('nthf,nthe->nhfe', feat_key, value_h, precision=highest)
    zero_state = jnp.zeros((1,) + local_state.shape[1:], jnp.float32)
    prior_state = jnp.concatenate([zero_state, jnp.cumsum(local_state, axis=0)[:-1]], axis=0)
    scores = jnp.einsum('nthf,nshf->nhts', feat_query, feat_key, precision=highest)
    attn_weights = rounded(jnp.where(causal, scores, 0.0))
    numerator = jnp.einsum('nhts,nshe->nthe', attn_weights, value_h, precision=highest)
    numerator = numerator + jnp.einsum('nthf,nhfe->nthe', feat_query, prior_state, precision=highest)
    inv_rms = lax.rsqrt(lax.optimization_barrier(jnp.mean(numerator * numerator, axis=-1, keepdims=True)) + norm_eps)
    normed = numerator * inv_rms
    gain_h = norm_gain.reshape(head_count, HEAD).astype(jnp.float32)
    grad_normed = grad_f * gain_h
    grad_numer = inv_rms * (grad_normed - normed * lax.optimization_barrier(jnp.mean(grad_normed * normed, axis=-1, keepdims=True)))
    grad_gain = lax.optimization_barrier(jnp.sum(normed * grad_f, axis=(0, 1))).reshape(width_all)
    numer_low = rounded(grad_numer)
    local_adjoint = jnp.einsum('nthf,nthe->nhfe', feat_query, numer_low, precision=highest)
    reverse_sum = jnp.cumsum(local_adjoint[::-1], axis=0)[::-1]
    later_state = jnp.concatenate([reverse_sum[1:], zero_state], axis=0)
    mixed = jnp.einsum('nthe,nshe->nhts', numer_low, value_h, precision=highest)
    mixed_low = rounded(jnp.where(causal, mixed, 0.0))
    grad_fq = jnp.einsum('nhts,nshf->nthf', mixed_low, feat_key, precision=highest)
    grad_fq = grad_fq + jnp.einsum('nthe,nhfe->nthf', grad_numer, prior_state, precision=highest)
    grad_fk = jnp.einsum('nhts,nthf->nshf', mixed_low, feat_query, precision=highest)
    grad_fk = grad_fk + jnp.einsum('nshe,nhfe->nshf', value_h, later_state, precision=highest)
    grad_v = jnp.einsum('nhts,nthe->nshe', attn_weights, numer_low, precision=highest)
    grad_v = grad_v + jnp.einsum('nshf,nhfe->nshe', feat_key, later_state, precision=highest)
    pre_grad_q = rounded(grad_fq * jnp.minimum(jnp.exp(pre_query), 1.0))
    pre_grad_k = rounded(grad_fk * jnp.minimum(jnp.exp(pre_key), 1.0))
    grad_query = jnp.einsum('nthe,hde->nthd', pre_grad_q, map_query, precision=highest)
    grad_key = jnp.einsum('nthe,hde->nthd', pre_grad_k, map_key, precision=highest)
    sum_wq = jnp.einsum('nthd,nthe->hde', query_h, pre_grad_q, precision=highest).reshape(width_all, HEAD)
    sum_wk = jnp.einsum('nthd,nthe->hde', key_h, pre_grad_k, precision=highest).reshape(width_all, HEAD)
    return (grad_query.reshape(length, width_all).astype(jnp.bfloat16), grad_key.reshape(length, width_all).astype(jnp.bfloat16), grad_v.reshape(length, width_all).astype(jnp.bfloat16), sum_wq, sum_wk, grad_gain)

def reference(query_in, key_in, value_in, grad_out, w_query, w_key, norm_gain):

    def per_sequence(items):
        return one_sequence(items[0], items[1], items[2], items[3], w_query, w_key, norm_gain)
    grad_query, grad_key, grad_value, sum_wq, sum_wk, sum_gain = lax.map(per_sequence, (query_in, key_in, value_in, grad_out))
    return (grad_query, grad_key, grad_value, lax.optimization_barrier(jnp.sum(sum_wq, axis=0)), lax.optimization_barrier(jnp.sum(sum_wk, axis=0)), lax.optimization_barrier(jnp.sum(sum_gain, axis=0)))
```

```python
import functools

import jax
import jax.numpy as jnp
from jax import lax
from jax.experimental import pallas as pl
from jax.experimental.pallas import tpu as pltpu
from jax.sharding import PartitionSpec as P

HEAD = 128
MESH = pl.DeviceIdType.MESH

norm_eps = 1e-05
highest = lax.Precision.HIGHEST


def scan_kernel(rows, reverse, local, out, peer, inbox, outbox, sx, rx, sy, ry):
    heads = local.shape[0]
    dp, seq = lax.axis_index("dp"), lax.axis_index("seq")
    y, half = seq // 2, seq % 2
    partner = y * 2 + (1 - half)
    step = rows - 1 if reverse else 1
    ahead = ((y + step) % rows) * 2 + half
    behind = ((y + rows - step) % rows) * 2 + half
    first, last = (rows - 1, 0) if reverse else (0, rows - 1)
    barrier = pltpu.get_barrier_semaphore()
    for other in (partner, ahead, behind):
        pl.semaphore_signal(barrier, inc=1, device_id=(dp, other), device_id_type=MESH)
    pl.semaphore_wait(barrier, 3)

    def across(h):
        return pltpu.make_async_remote_copy(
            src_ref=local.at[h], dst_ref=peer.at[h], send_sem=sx.at[h], recv_sem=rx.at[h],
            device_id=(dp, partner), device_id_type=MESH)

    def along(h):
        return pltpu.make_async_remote_copy(
            src_ref=outbox.at[h], dst_ref=inbox.at[h], send_sem=sy.at[h], recv_sem=ry.at[h],
            device_id=(dp, ahead), device_id_type=MESH)

    @pl.loop(0, heads)
    def _(h):
        across(h).start()

    @pl.when(y == first)
    def _():
        inbox[...] = jnp.zeros_like(inbox)

    pick = jnp.where(half == (0 if reverse else 1), 1.0, 0.0).astype(jnp.float32)

    @pl.loop(0, heads)
    def _(h):
        across(h).wait_recv()

        @pl.when(y != first)
        def _():
            along(h).wait_recv()

        outbox[h] = inbox[h] + (local[h] + peer[h])
        out[h] = inbox[h] + pick * peer[h]

        @pl.when(y != last)
        def _():
            along(h).start()

    @pl.loop(0, heads)
    def _(h):
        across(h).wait_send()

        @pl.when(y != last)
        def _():
            along(h).wait_send()


def scan_states(state, reverse, rows, name, number):
    heads = state.shape[0]
    whole = pltpu.VMEM(state.shape, jnp.float32)
    dma = pltpu.SemaphoreType.DMA((heads,))
    return pl.pallas_call(
        functools.partial(scan_kernel, rows, reverse),
        out_shape=jax.ShapeDtypeStruct(state.shape, jnp.float32),
        in_specs=[pl.BlockSpec(memory_space=pltpu.VMEM)],
        out_specs=pl.BlockSpec(memory_space=pltpu.VMEM),
        scratch_shapes=[whole, whole, whole, dma, dma, dma, dma],
        compiler_params=pltpu.CompilerParams(collective_id=number, has_side_effects=True),
        name=name,
    )(state)


def reduce_kernel(depth, rows, part, out, rcore, summed, rz, block, rlo, slim, ry, mine, rhi, full,
                  score, kcore, sz, kz, slo, klo, sy, ky, syg, kyg, shi, khi, sg, kg):
    dp, seq = lax.axis_index("dp"), lax.axis_index("seq")
    z, low, core = dp // 4, (dp // 2) % 2, dp % 2
    y, half = seq // 2, seq % 2

    def to_z(k):
        return (((z + k) % depth) * 4 + low * 2 + core, seq)

    def to_y(k):
        return (dp, ((y + k) % rows) * 2 + half)

    to_core = (z * 4 + low * 2 + (1 - core), seq)
    to_low = (z * 4 + (1 - low) * 2 + core, seq)
    to_half = (dp, y * 2 + (1 - half))
    barrier = pltpu.get_barrier_semaphore()
    others = [to_core, to_low, to_half]
    others += [to_z(k) for k in range(1, depth)] + [to_y(k) for k in range(1, rows)]
    for other in others:
        pl.semaphore_signal(barrier, inc=1, device_id=other, device_id_type=MESH)
    pl.semaphore_wait(barrier, len(others))

    def send(src, dst, s, r, device):
        return pltpu.make_async_remote_copy(
            src_ref=src, dst_ref=dst, send_sem=s, recv_sem=r, device_id=device, device_id_type=MESH)

    def core_copy(k):
        at = (z + k) % depth
        return send(part.at[1 - core, at], rcore.at[k], score.at[k], kcore.at[k], to_core)

    def z_copy(k):
        return send(summed.at[k], rz.at[k], sz.at[k], kz.at[k], to_z(k))

    @pl.loop(1, depth + 1)
    def _(k):
        core_copy(k % depth).start()

    @pl.loop(1, depth)
    def _(k):
        core_copy(k).wait_recv()
        summed[k] = part[core, (z + k) % depth] + rcore[k]
        z_copy(k).start()

    core_copy(0).wait_recv()
    block[...] = part[core, z] + rcore[0]

    @pl.loop(1, depth)
    def _(k):
        z_copy(k).wait_recv()
        block[...] += rz[k]

    low_copy = send(block.at[1 - low], rlo, slo, klo, to_low)
    low_copy.start()
    low_copy.wait_recv()
    slim[...] = block[low] + rlo[...]

    def y_copy(k):
        at = (y + k) % rows
        return send(slim.at[pl.ds(2 * at, 2)], ry.at[k, pl.ds(0, 2)], sy.at[k], ky.at[k], to_y(k))

    def gain_copy(k):
        return send(slim.at[pl.ds(2 * rows, 1)], ry.at[k, pl.ds(2, 1)], syg.at[k], kyg.at[k], to_y(k))

    @pl.loop(1, rows)
    def _(k):
        y_copy(k).start()
        gain_copy(k).start()

    mine[pl.ds(0, 2)] = slim[pl.ds(2 * y, 2)]
    mine[pl.ds(2, 1)] = slim[pl.ds(2 * rows, 1)]

    @pl.loop(1, rows)
    def _(k):
        y_copy(k).wait_recv()
        gain_copy(k).wait_recv()
        mine[...] += ry[k]

    half_copy = send(mine, rhi, shi, khi, to_half)
    half_copy.start()
    half_copy.wait()
    mine[...] += rhi[...]

    def gather_copy(k):
        return send(mine.at[pl.ds(0, 2)], full.at[pl.ds(2 * y, 2)], sg.at[k], kg.at[k], to_y(k))

    @pl.loop(1, rows)
    def _(k):
        gather_copy(k).start()

    def arrival(k):
        at = (y + rows - k) % rows
        return send(mine.at[pl.ds(0, 2)], full.at[pl.ds(2 * at, 2)], sg.at[k], kg.at[k], to_y(k))

    @pl.loop(1, rows)
    def _(k):
        at = (y + rows - k) % rows
        arrival(k).wait_recv()
        out[pl.ds(2 * at, 2)] = full[pl.ds(2 * at, 2)]

    out[pl.ds(2 * y, 2)] = mine[pl.ds(0, 2)]
    out[pl.ds(2 * rows, 1)] = mine[pl.ds(2, 1)]

    core_copy(0).wait_send()
    low_copy.wait_send()

    @pl.loop(1, depth)
    def _(k):
        core_copy(k).wait_send()
        z_copy(k).wait_send()

    @pl.loop(1, rows)
    def _(k):
        y_copy(k).wait_send()
        gain_copy(k).wait_send()
        gather_copy(k).wait_send()


def reduce_gradients(sum_wq, sum_wk, sum_gain, depth, rows):
    owners = depth * 4
    own = sum_wq.shape[0] // owners
    tiles = own // 8
    both = jnp.stack(
        [sum_wq.reshape(owners, tiles, 8, HEAD), sum_wk.reshape(owners, tiles, 8, HEAD)], axis=2)
    both = both.reshape(owners, 2 * tiles, 8, HEAD)
    gains = jnp.pad(sum_gain.reshape(owners, 1, 1, own), ((0, 0), (0, 0), (0, 7), (0, HEAD - own)))
    part = jnp.concatenate([both, gains], axis=1)
    count = 2 * tiles + 1
    part = part.reshape(depth, 2, 2, count, 8, HEAD).transpose(2, 0, 1, 3, 4, 5)
    dma = pltpu.SemaphoreType.DMA

    def f32(*shape):
        return pltpu.VMEM(shape + (8, HEAD), jnp.float32)

    total = pl.pallas_call(
        functools.partial(reduce_kernel, depth, rows),
        out_shape=jax.ShapeDtypeStruct((count, 8, HEAD), jnp.float32),
        in_specs=[pl.BlockSpec(memory_space=pltpu.VMEM)],
        out_specs=pl.BlockSpec(memory_space=pltpu.VMEM),
        scratch_shapes=[
            f32(depth, 2, count), f32(depth, 2, count), f32(depth, 2, count), f32(2, count), f32(count),
            f32(count), f32(rows, 3), f32(3), f32(3), f32(count),
            dma((depth,)), dma((depth,)), dma((depth,)), dma((depth,)), dma, dma,
            dma((rows,)), dma((rows,)), dma((rows,)), dma((rows,)), dma, dma, dma((rows,)), dma((rows,)),
        ],
        compiler_params=pltpu.CompilerParams(collective_id=2, has_side_effects=True),
        name="reduce_gradients",
    )(part)
    pairs = total[: 2 * tiles].reshape(tiles, 2, 8, HEAD)
    return pairs[:, 0].reshape(own, HEAD), pairs[:, 1].reshape(own, HEAD), total[2 * tiles, 0, :own]


def per_device(depth, rows, query_in, key_in, value_in, grad_out, w_query, w_key, norm_gain):
    seq_count, tok_rows, width_all = query_in.shape
    head_count = width_all // HEAD

    def split_heads(tensor):
        return tensor.reshape(seq_count, tok_rows, head_count, HEAD)

    query_h = split_heads(query_in)
    key_h = split_heads(key_in)
    value_h = split_heads(value_in)
    grad_h = split_heads(grad_out)
    map_query = w_query.reshape(head_count, HEAD, HEAD)
    map_key = w_key.reshape(head_count, HEAD, HEAD)
    pre_query = jnp.einsum("bthd,hde->bthe", query_h, map_query, preferred_element_type=jnp.float32)
    pre_key = jnp.einsum("bthd,hde->bthe", key_h, map_key, preferred_element_type=jnp.float32)
    feat_query = (jax.nn.elu(pre_query) + 1.0).astype(jnp.bfloat16)
    feat_key = (jax.nn.elu(pre_key) + 1.0).astype(jnp.bfloat16)
    position = lax.broadcasted_iota(jnp.int32, (tok_rows, tok_rows), 0)
    column = lax.broadcasted_iota(jnp.int32, (tok_rows, tok_rows), 1)
    causal = position >= column
    local_state = jnp.einsum(
        "bthf,bthe->bhfe", feat_key, value_h, preferred_element_type=jnp.float32
    )
    scores = jnp.einsum("bthf,bshf->bhts", feat_query, feat_key, preferred_element_type=jnp.float32)
    attn_weights = jnp.where(causal, scores, 0.0).astype(jnp.bfloat16)
    inner_sum = jnp.einsum(
        "bhts,bshe->bthe", attn_weights, value_h, preferred_element_type=jnp.float32
    )
    prior_state = scan_states(local_state[0], False, rows, "prior_scan", 0)[None]
    query_wide = feat_query.astype(jnp.float32)
    numerator = inner_sum + jnp.einsum(
        "bthf,bhfe->bthe", query_wide, prior_state, precision=highest
    )
    inv_rms = lax.rsqrt(jnp.mean(numerator * numerator, axis=-1, keepdims=True) + norm_eps)
    normed = numerator * inv_rms
    gain_h = norm_gain.reshape(head_count, HEAD)
    grad_f = grad_h.astype(jnp.float32)
    grad_normed = grad_f * gain_h
    grad_numer = inv_rms * (
        grad_normed - normed * jnp.mean(grad_normed * normed, axis=-1, keepdims=True)
    )
    grad_gain = jnp.sum(normed * grad_f, axis=(0, 1)).reshape(width_all)
    numer_low = grad_numer.astype(jnp.bfloat16)
    local_adjoint = jnp.einsum(
        "bthf,bthe->bhfe", feat_query, numer_low, preferred_element_type=jnp.float32
    )
    mixed = jnp.einsum("bthe,bshe->bhts", numer_low, value_h, preferred_element_type=jnp.float32)
    mixed_low = jnp.where(causal, mixed, 0.0).astype(jnp.bfloat16)
    grad_fq = jnp.einsum("bhts,bshf->bthf", mixed_low, feat_key, preferred_element_type=jnp.float32)
    grad_fq = grad_fq + jnp.einsum("bthe,bhfe->bthf", grad_numer, prior_state, precision=highest)
    slope_query = jnp.minimum(jnp.exp(pre_query), 1.0)
    pre_grad_q = (grad_fq * slope_query).astype(jnp.bfloat16)
    grad_query = jnp.einsum(
        "bthe,hde->bthd", pre_grad_q, map_query, preferred_element_type=jnp.float32
    )
    sum_wq = jnp.einsum("bthd,bthe->hde", query_h, pre_grad_q, preferred_element_type=jnp.float32)
    later_state = scan_states(local_adjoint[0], True, rows, "later_scan", 1)[None]
    grad_fk = jnp.einsum(
        "bhts,bthf->bshf", mixed_low, feat_query, preferred_element_type=jnp.float32
    )
    grad_fk = grad_fk + jnp.einsum(
        "bshe,bhfe->bshf", value_h.astype(jnp.float32), later_state, precision=highest
    )
    grad_v = jnp.einsum(
        "bhts,bthe->bshe", attn_weights, numer_low, preferred_element_type=jnp.float32
    )
    grad_v = grad_v + jnp.einsum(
        "bshf,bhfe->bshe", feat_key.astype(jnp.float32), later_state, precision=highest
    )
    slope_key = jnp.minimum(jnp.exp(pre_key), 1.0)
    pre_grad_k = (grad_fk * slope_key).astype(jnp.bfloat16)
    grad_key = jnp.einsum("bthe,hde->bthd", pre_grad_k, map_key, preferred_element_type=jnp.float32)
    sum_wk = jnp.einsum("bthd,bthe->hde", key_h, pre_grad_k, preferred_element_type=jnp.float32)
    sum_wq = sum_wq.reshape(width_all, HEAD)
    sum_wk = sum_wk.reshape(width_all, HEAD)
    total_wq, total_wk, total_gain = reduce_gradients(sum_wq, sum_wk, grad_gain, depth, rows)
    out_shape = (seq_count, tok_rows, width_all)
    return (
        grad_query.astype(jnp.bfloat16).reshape(out_shape),
        grad_key.astype(jnp.bfloat16).reshape(out_shape),
        grad_v.astype(jnp.bfloat16).reshape(out_shape),
        total_wq,
        total_wk,
        total_gain,
    )


def solution(mesh):
    tokens = P("dp", "seq", None)
    body = functools.partial(per_device, mesh.shape["dp"] // 4, mesh.shape["seq"] // 2)
    return jax.shard_map(
        body,
        mesh=mesh,
        in_specs=(tokens, tokens, tokens, tokens, P(), P(), P()),
        out_specs=(tokens, tokens, tokens, P("dp", None), P("dp", None), P("dp")),
        check_vma=False,
    )
```

```python
import functools

import jax
import jax.numpy as jnp
from jax import lax
from jax.experimental import pallas as pl
from jax.experimental.pallas import tpu as pltpu
from jax.sharding import PartitionSpec as P

HEAD = 128
MESH = pl.DeviceIdType.MESH

norm_eps = 1e-05


def product(left, right, over):
    return lax.dot_general(left, right, ((over[:1], over[1:]), ((), ())), preferred_element_type=jnp.float32)


def two_terms(wide):
    high = wide.astype(jnp.bfloat16)
    return high, (wide - high.astype(jnp.float32)).astype(jnp.bfloat16)


def exchange(src, dst, send_sem, recv_sem, device):
    return pltpu.make_async_remote_copy(
        src_ref=src, dst_ref=dst, send_sem=send_sem, recv_sem=recv_sem, device_id=device, device_id_type=MESH)


def attention_kernel(rows, query, key, value, cotangent, wq, wk, gain, grad_query, grad_key, grad_value, part,
                     local, peer, inbox, outbox, adjoint, peer_adj, inbox_adj, outbox_adj,
                     feat_k, slope_k, part_fk, part_v, sx, rx, sy, ry, sx2, rx2, sy2, ry2):
    heads = local.shape[0]
    dp, seq = lax.axis_index("dp"), lax.axis_index("seq")
    y, half = seq // 2, seq % 2
    top = rows - 1
    partner = (dp, y * 2 + (1 - half))
    above = (dp, ((y + 1) % rows) * 2 + half)
    below = (dp, ((y + rows - 1) % rows) * 2 + half)
    barrier = pltpu.get_barrier_semaphore()
    for other in (partner, above, below):
        pl.semaphore_signal(barrier, inc=1, device_id=other, device_id_type=MESH)
    pl.semaphore_wait(barrier, 3)

    def across(h):
        return exchange(local.at[h], peer.at[h], sx.at[h], rx.at[h], partner)

    def upward(h):
        return exchange(outbox.at[h], inbox.at[h], sy.at[h], ry.at[h], above)

    def across_adj(h):
        return exchange(adjoint.at[h], peer_adj.at[h], sx2.at[h], rx2.at[h], partner)

    def downward(h):
        return exchange(outbox_adj.at[h], inbox_adj.at[h], sy2.at[h], ry2.at[h], below)

    def columns(h):
        return pl.ds(pl.multiple_of(h * HEAD, HEAD), HEAD)

    tokens = query.shape[0]
    position = lax.broadcasted_iota(jnp.int32, (tokens, tokens), 0)
    column = lax.broadcasted_iota(jnp.int32, (tokens, tokens), 1)
    causal = position >= column

    def put_sums(h, which, total):
        own = HEAD // 2
        for core in range(2):
            for tile in range(own // 8):
                start = core * own + tile * 8
                part[core, h // 2, h % 2, 2 * tile + which] = total[start : start + 8]

    @pl.loop(0, heads)
    def _(h):
        at = columns(h)
        pre = product(key[:, at], wk[at, :], (1, 0))
        slope = jnp.exp(jnp.minimum(pre, 0.0))
        feat = jnp.where(pre > 0.0, pre + 1.0, slope).astype(jnp.bfloat16)
        slope_k[h] = slope
        feat_k[h] = feat
        local[h] = product(feat, value[:, at], (0, 0))

        @pl.when(h > 0)
        def _():
            across(h - 1).start()

    @pl.when(y == 0)
    def _():
        inbox[...] = jnp.zeros_like(inbox)

    @pl.when(y == top)
    def _():
        inbox_adj[...] = jnp.zeros_like(inbox_adj)

    across(heads - 1).start()
    is_second = jnp.where(half == 1, 1.0, 0.0).astype(jnp.float32)

    def forward(h):
        at = columns(h)
        fk, v = feat_k[h], value[:, at]
        q, wq_h = query[:, at], wq[at, :]
        pre = product(q, wq_h, (1, 0))
        slope = jnp.exp(jnp.minimum(pre, 0.0))
        fq = jnp.where(pre > 0.0, pre + 1.0, slope).astype(jnp.bfloat16)
        attn = jnp.where(causal, product(fq, fk, (1, 1)), 0.0).astype(jnp.bfloat16)
        inner = product(attn, v, (1, 0))
        across(h).wait_recv()

        @pl.when(y != 0)
        def _():
            upward(h).wait_recv()

        outbox[h] = inbox[h] + (local[h] + peer[h])
        state_high, state_low = two_terms(inbox[h] + is_second * peer[h])

        @pl.when(y != top)
        def _():
            upward(h).start()

        numerator = inner + (product(fq, state_high, (1, 0)) + product(fq, state_low, (1, 0)))
        inv_rms = lax.rsqrt(jnp.mean(numerator * numerator, axis=-1, keepdims=True) + norm_eps)
        normed = numerator * inv_rms
        grad = cotangent[:, at].astype(jnp.float32)
        grad_normed = grad * gain[:, at]
        grad_numer = inv_rms * (
            grad_normed - normed * jnp.mean(grad_normed * normed, axis=-1, keepdims=True))
        low, rest = two_terms(grad_numer)
        adjoint[h] = product(fq, low, (0, 0))
        mixed = jnp.where(causal, product(low, v, (1, 1)), 0.0).astype(jnp.bfloat16)
        grad_fq = product(mixed, fk, (1, 0)) + (
            product(low, state_high, (1, 1)) + (product(low, state_low, (1, 1)) + product(rest, state_high, (1, 1))))
        across_adj(h).start()
        pre_grad = (grad_fq * slope).astype(jnp.bfloat16)
        grad_query[:, at] = product(pre_grad, wq_h, (1, 1)).astype(jnp.bfloat16)
        part_fk[h] = product(mixed, fq, (0, 0))
        part_v[h] = product(attn, low, (0, 0))
        put_sums(h, 0, product(q, pre_grad, (0, 0)))
        gains = jnp.broadcast_to(jnp.sum(normed * grad, axis=0, keepdims=True), (8, HEAD))
        for core in range(2):
            part[core, h // 2, h % 2, HEAD // 8] = gains

    def backward(h):
        at = columns(h)
        across_adj(h).wait_recv()

        @pl.when(y != top)
        def _():
            downward(h).wait_recv()

        outbox_adj[h] = inbox_adj[h] + (adjoint[h] + peer_adj[h])
        state_high, state_low = two_terms(inbox_adj[h] + (1.0 - is_second) * peer_adj[h])

        @pl.when(y != 0)
        def _():
            downward(h).start()

        v, fk, wk_h = value[:, at], feat_k[h], wk[at, :]
        grad_fk = part_fk[h] + (product(v, state_high, (1, 1)) + product(v, state_low, (1, 1)))
        pre_grad = (grad_fk * slope_k[h]).astype(jnp.bfloat16)
        grad_v = part_v[h] + (product(fk, state_high, (1, 0)) + product(fk, state_low, (1, 0)))
        grad_value[:, at] = grad_v.astype(jnp.bfloat16)
        grad_key[:, at] = product(pre_grad, wk_h, (1, 1)).astype(jnp.bfloat16)
        put_sums(h, 1, product(key[:, at], pre_grad, (0, 0)))

    lag = 3 * (top - y)

    @pl.loop(0, heads + 3 * top)
    def _(step):
        @pl.when(step < heads)
        def _():
            forward(step)

        @pl.when(step >= lag)
        def _():
            @pl.when(step < lag + heads)
            def _():
                backward(step - lag)

    @pl.loop(0, heads)
    def _(h):
        across(h).wait_send()
        across_adj(h).wait_send()

        @pl.when(y != top)
        def _():
            upward(h).wait_send()

        @pl.when(y != 0)
        def _():
            downward(h).wait_send()


def attention(query, key, value, cotangent, wq, wk, gain, depth, rows):
    heads = wq.shape[0] // HEAD
    tokens, width = query.shape
    states = pltpu.VMEM((heads, HEAD, HEAD), jnp.float32)
    dma = pltpu.SemaphoreType.DMA((heads,))
    vmem = pl.BlockSpec(memory_space=pltpu.VMEM)
    grads = jax.ShapeDtypeStruct((tokens, width), jnp.bfloat16)
    return pl.pallas_call(
        functools.partial(attention_kernel, rows),
        out_shape=(grads, grads, grads,
                   jax.ShapeDtypeStruct((2, depth, 2, HEAD // 8 + 1, 8, HEAD), jnp.float32)),
        in_specs=[vmem] * 7,
        out_specs=(vmem,) * 4,
        scratch_shapes=[states] * 8
        + [pltpu.VMEM((heads, tokens, HEAD), jnp.bfloat16), pltpu.VMEM((heads, tokens, HEAD), jnp.float32)]
        + [pltpu.VMEM((heads, tokens, HEAD), jnp.float32)] * 2
        + [dma] * 8,
        compiler_params=pltpu.CompilerParams(collective_id=0, has_side_effects=True),
        name="attention",
    )(query, key, value, cotangent, wq, wk, gain)


def reduce_kernel(depth, rows, part, out, rcore, summed, rz, block, rlo, slim, ry, mine, rhi, full,
                  score, kcore, sz, kz, slo, klo, sy, ky, syg, kyg, shi, khi, sg, kg):
    dp, seq = lax.axis_index("dp"), lax.axis_index("seq")
    z, low, core = dp // 4, (dp // 2) % 2, dp % 2
    y, half = seq // 2, seq % 2

    def to_z(k):
        return (((z + k) % depth) * 4 + low * 2 + core, seq)

    def to_y(k):
        return (dp, ((y + k) % rows) * 2 + half)

    to_core = (z * 4 + low * 2 + (1 - core), seq)
    to_low = (z * 4 + (1 - low) * 2 + core, seq)
    to_half = (dp, y * 2 + (1 - half))
    barrier = pltpu.get_barrier_semaphore()
    others = [to_core, to_low, to_half]
    others += [to_z(k) for k in range(1, depth)] + [to_y(k) for k in range(1, rows)]
    for other in others:
        pl.semaphore_signal(barrier, inc=1, device_id=other, device_id_type=MESH)
    pl.semaphore_wait(barrier, len(others))

    def send(src, dst, s, r, device):
        return pltpu.make_async_remote_copy(
            src_ref=src, dst_ref=dst, send_sem=s, recv_sem=r, device_id=device, device_id_type=MESH)

    def core_copy(k):
        at = (z + k) % depth
        return send(part.at[1 - core, at], rcore.at[k], score.at[k], kcore.at[k], to_core)

    def z_copy(k):
        return send(summed.at[k], rz.at[k], sz.at[k], kz.at[k], to_z(k))

    @pl.loop(1, depth + 1)
    def _(k):
        core_copy(k % depth).start()

    @pl.loop(1, depth)
    def _(k):
        core_copy(k).wait_recv()
        summed[k] = part[core, (z + k) % depth] + rcore[k]
        z_copy(k).start()

    core_copy(0).wait_recv()
    block[...] = part[core, z] + rcore[0]

    @pl.loop(1, depth)
    def _(k):
        z_copy(k).wait_recv()
        block[...] += rz[k]

    low_copy = send(block.at[1 - low], rlo, slo, klo, to_low)
    low_copy.start()
    low_copy.wait_recv()
    slim[...] = block[low] + rlo[...]

    def y_copy(k):
        at = (y + k) % rows
        return send(slim.at[pl.ds(2 * at, 2)], ry.at[k, pl.ds(0, 2)], sy.at[k], ky.at[k], to_y(k))

    def gain_copy(k):
        return send(slim.at[pl.ds(2 * rows, 1)], ry.at[k, pl.ds(2, 1)], syg.at[k], kyg.at[k], to_y(k))

    @pl.loop(1, rows)
    def _(k):
        y_copy(k).start()
        gain_copy(k).start()

    mine[pl.ds(0, 2)] = slim[pl.ds(2 * y, 2)]
    mine[pl.ds(2, 1)] = slim[pl.ds(2 * rows, 1)]

    @pl.loop(1, rows)
    def _(k):
        y_copy(k).wait_recv()
        gain_copy(k).wait_recv()
        mine[...] += ry[k]

    half_copy = send(mine, rhi, shi, khi, to_half)
    half_copy.start()
    half_copy.wait()
    mine[...] += rhi[...]

    def gather_copy(k):
        return send(mine.at[pl.ds(0, 2)], full.at[pl.ds(2 * y, 2)], sg.at[k], kg.at[k], to_y(k))

    @pl.loop(1, rows)
    def _(k):
        gather_copy(k).start()

    def arrival(k):
        at = (y + rows - k) % rows
        return send(mine.at[pl.ds(0, 2)], full.at[pl.ds(2 * at, 2)], sg.at[k], kg.at[k], to_y(k))

    @pl.loop(1, rows)
    def _(k):
        at = (y + rows - k) % rows
        arrival(k).wait_recv()
        out[pl.ds(2 * at, 2)] = full[pl.ds(2 * at, 2)]

    out[pl.ds(2 * y, 2)] = mine[pl.ds(0, 2)]
    out[pl.ds(2 * rows, 1)] = mine[pl.ds(2, 1)]

    core_copy(0).wait_send()
    low_copy.wait_send()

    @pl.loop(1, depth)
    def _(k):
        core_copy(k).wait_send()
        z_copy(k).wait_send()

    @pl.loop(1, rows)
    def _(k):
        y_copy(k).wait_send()
        gain_copy(k).wait_send()
        gather_copy(k).wait_send()


def reduce_gradients(part, depth, rows):
    count = part.shape[3]
    dma = pltpu.SemaphoreType.DMA

    def f32(*shape):
        return pltpu.VMEM(shape + (8, HEAD), jnp.float32)

    return pl.pallas_call(
        functools.partial(reduce_kernel, depth, rows),
        out_shape=jax.ShapeDtypeStruct((count, 8, HEAD), jnp.float32),
        in_specs=[pl.BlockSpec(memory_space=pltpu.VMEM)],
        out_specs=pl.BlockSpec(memory_space=pltpu.VMEM),
        scratch_shapes=[
            f32(depth, 2, count), f32(depth, 2, count), f32(depth, 2, count), f32(2, count), f32(count),
            f32(count), f32(rows, 3), f32(3), f32(3), f32(count),
            dma((depth,)), dma((depth,)), dma((depth,)), dma((depth,)), dma, dma,
            dma((rows,)), dma((rows,)), dma((rows,)), dma((rows,)), dma, dma, dma((rows,)), dma((rows,)),
        ],
        compiler_params=pltpu.CompilerParams(collective_id=2, has_side_effects=True),
        name="reduce_gradients",
    )(part)


def per_device(depth, rows, query_in, key_in, value_in, grad_out, w_query, w_key, norm_gain):
    width_all = query_in.shape[2]
    grad_query, grad_key, grad_value, part = attention(
        query_in[0], key_in[0], value_in[0], grad_out[0], w_query, w_key, norm_gain.reshape(1, width_all), depth, rows)
    total = reduce_gradients(part, depth, rows)
    own = HEAD // 2
    pairs = total[:-1].reshape(own // 8, 2, 8, HEAD)
    gains = total[-1, 0].reshape(2, own)
    total_gain = jnp.where(lax.axis_index("dp") % 2 == 0, gains[0], gains[1])
    return (
        grad_query[None],
        grad_key[None],
        grad_value[None],
        pairs[:, 0].reshape(own, HEAD),
        pairs[:, 1].reshape(own, HEAD),
        total_gain,
    )


def solution(mesh):
    tokens = P("dp", "seq", None)
    body = functools.partial(per_device, mesh.shape["dp"] // 4, mesh.shape["seq"] // 2)
    return jax.shard_map(
        body,
        mesh=mesh,
        in_specs=(tokens, tokens, tokens, tokens, P(), P(), P()),
        out_specs=(tokens, tokens, tokens, P("dp", None), P("dp", None), P("dp")),
        check_vma=False,
    )
```

```python
import functools

import jax
import jax.numpy as jnp
from jax import lax
from jax.experimental import pallas as pl
from jax.experimental.pallas import tpu as pltpu
from jax.sharding import PartitionSpec as P

HEAD = 128
MESH = pl.DeviceIdType.MESH

norm_eps = 1e-05


def product(left, right, over):
    return lax.dot_general(left, right, ((over[:1], over[1:]), ((), ())), preferred_element_type=jnp.float32)


def two_terms(wide):
    high = wide.astype(jnp.bfloat16)
    return high, (wide - high.astype(jnp.float32)).astype(jnp.bfloat16)


def exchange(src, dst, send_sem, recv_sem, device):
    return pltpu.make_async_remote_copy(
        src_ref=src, dst_ref=dst, send_sem=send_sem, recv_sem=recv_sem, device_id=device, device_id_type=MESH)


def attention_kernel(depth, rows, query, key, value, cotangent, wq, wk, gain, grad_query, grad_key, grad_value, out,
                     local, peer, inbox, outbox, adjoint, peer_adj, inbox_adj, outbox_adj,
                     feat_k, slope_k, part_fk, part_v, parts, rcore, summed, rz, block, rlo, slim, rrow, mine, rhi, full,
                     sx, rx, sy, ry, sx2, rx2, sy2, ry2, score, kcore, sz, kz,
                     slo, klo, srow, krow, srowg, krowg, shi, khi, sg, kg):
    heads = local.shape[0]
    dp, seq = lax.axis_index("dp"), lax.axis_index("seq")
    y, half = seq // 2, seq % 2
    top = rows - 1
    z, low, core = dp // 4, (dp // 2) % 2, dp % 2

    def to_z(k):
        return (((z + k) % depth) * 4 + low * 2 + core, seq)

    def to_y(k):
        return (dp, ((y + k) % rows) * 2 + half)

    to_core = (z * 4 + low * 2 + (1 - core), seq)
    to_low = (z * 4 + (1 - low) * 2 + core, seq)
    partner = (dp, y * 2 + (1 - half))
    above, below = to_y(1), to_y(rows - 1)
    barrier = pltpu.get_barrier_semaphore()
    others = [to_core, to_low, partner]
    others += [to_z(k) for k in range(1, depth)] + [to_y(k) for k in range(1, rows)]
    for other in others:
        pl.semaphore_signal(barrier, inc=1, device_id=other, device_id_type=MESH)
    pl.semaphore_wait(barrier, len(others))

    def across(h):
        return exchange(local.at[h], peer.at[h], sx.at[h], rx.at[h], partner)

    def upward(h):
        return exchange(outbox.at[h], inbox.at[h], sy.at[h], ry.at[h], above)

    def across_adj(h):
        return exchange(adjoint.at[h], peer_adj.at[h], sx2.at[h], rx2.at[h], partner)

    def downward(h):
        return exchange(outbox_adj.at[h], inbox_adj.at[h], sy2.at[h], ry2.at[h], below)

    def columns(h):
        return pl.ds(pl.multiple_of(((h + 2 * z) % heads) * HEAD, HEAD), HEAD)

    tiles = HEAD // 16
    sent = (pl.ds(0, tiles + 1), pl.ds(0, tiles))

    def core_copy(which, h):
        return exchange(parts.at[which, 1 - core, h, sent[which]], rcore.at[which, h, sent[which]],
                        score.at[which, h], kcore.at[which, h], to_core)

    def z_copy(which, h):
        return exchange(summed.at[which, h, sent[which]], rz.at[which, h, sent[which]],
                        sz.at[which, h], kz.at[which, h], to_z(h // 2))

    def relay(which, h):
        core_copy(which, h).wait_recv()
        summed[which, h, sent[which]] = parts[which, core, h, sent[which]] + rcore[which, h, sent[which]]

        @pl.when(h >= 2)
        def _():
            z_copy(which, h).start()

    tokens = query.shape[0]
    position = lax.broadcasted_iota(jnp.int32, (tokens, tokens), 0)
    column = lax.broadcasted_iota(jnp.int32, (tokens, tokens), 1)
    causal = position >= column

    def put_sums(h, which, total):
        own = HEAD // 2
        for side in range(2):
            parts[which, side, h, pl.ds(0, tiles)] = total[side * own : (side + 1) * own].reshape(tiles, 8, HEAD)

    @pl.loop(0, heads)
    def _(h):
        at = columns(h)
        pre = product(key[:, at], wk[at, :], (1, 0))
        slope = jnp.exp(jnp.minimum(pre, 0.0))
        feat = jnp.where(pre > 0.0, pre + 1.0, slope).astype(jnp.bfloat16)
        slope_k[h] = slope
        feat_k[h] = feat
        local[h] = product(feat, value[:, at], (0, 0))

        @pl.when(h > 0)
        def _():
            across(h - 1).start()

    @pl.when(y == 0)
    def _():
        inbox[...] = jnp.zeros_like(inbox)

    @pl.when(y == top)
    def _():
        inbox_adj[...] = jnp.zeros_like(inbox_adj)

    across(heads - 1).start()
    is_second = jnp.where(half == 1, 1.0, 0.0).astype(jnp.float32)

    def forward(h):
        at = columns(h)
        fk, v = feat_k[h], value[:, at]
        q, wq_h = query[:, at], wq[at, :]
        pre = product(q, wq_h, (1, 0))
        slope = jnp.exp(jnp.minimum(pre, 0.0))
        fq = jnp.where(pre > 0.0, pre + 1.0, slope).astype(jnp.bfloat16)
        attn = jnp.where(causal, product(fq, fk, (1, 1)), 0.0).astype(jnp.bfloat16)
        inner = product(attn, v, (1, 0))
        across(h).wait_recv()

        @pl.when(y != 0)
        def _():
            upward(h).wait_recv()

        outbox[h] = inbox[h] + (local[h] + peer[h])
        state_high, state_low = two_terms(inbox[h] + is_second * peer[h])

        @pl.when(y != top)
        def _():
            upward(h).start()

        numerator = inner + (product(fq, state_high, (1, 0)) + product(fq, state_low, (1, 0)))
        inv_rms = lax.rsqrt(jnp.mean(numerator * numerator, axis=-1, keepdims=True) + norm_eps)
        normed = numerator * inv_rms
        grad = cotangent[:, at].astype(jnp.float32)
        grad_normed = grad * gain[:, at]
        grad_numer = inv_rms * (
            grad_normed - normed * jnp.mean(grad_normed * normed, axis=-1, keepdims=True))
        low_numer, rest = two_terms(grad_numer)
        adjoint[h] = product(fq, low_numer, (0, 0))
        mixed = jnp.where(causal, product(low_numer, v, (1, 1)), 0.0).astype(jnp.bfloat16)
        grad_fq = product(mixed, fk, (1, 0)) + (
            product(low_numer, state_high, (1, 1)) + (product(low_numer, state_low, (1, 1)) + product(rest, state_high, (1, 1))))
        across_adj(h).start()
        pre_grad = (grad_fq * slope).astype(jnp.bfloat16)
        grad_query[:, at] = product(pre_grad, wq_h, (1, 1)).astype(jnp.bfloat16)
        put_sums(h, 0, product(q, pre_grad, (0, 0)))
        gains = jnp.broadcast_to(jnp.sum(normed * grad, axis=0, keepdims=True), (8, HEAD))
        for side in range(2):
            parts[0, side, h, tiles] = gains
        part_fk[h] = product(mixed, fq, (0, 0))
        part_v[h] = product(attn, low_numer, (0, 0))
        core_copy(0, h).start()

    def backward(h):
        at = columns(h)
        across_adj(h).wait_recv()

        @pl.when(y != top)
        def _():
            downward(h).wait_recv()

        outbox_adj[h] = inbox_adj[h] + (adjoint[h] + peer_adj[h])
        state_high, state_low = two_terms(inbox_adj[h] + (1.0 - is_second) * peer_adj[h])

        @pl.when(y != 0)
        def _():
            downward(h).start()

        v, fk, wk_h = value[:, at], feat_k[h], wk[at, :]
        grad_fk = part_fk[h] + (product(v, state_high, (1, 1)) + product(v, state_low, (1, 1)))
        pre_grad = (grad_fk * slope_k[h]).astype(jnp.bfloat16)
        grad_v = part_v[h] + (product(fk, state_high, (1, 0)) + product(fk, state_low, (1, 0)))
        put_sums(h, 1, product(key[:, at], pre_grad, (0, 0)))
        grad_value[:, at] = grad_v.astype(jnp.bfloat16)
        grad_key[:, at] = product(pre_grad, wk_h, (1, 1)).astype(jnp.bfloat16)
        core_copy(1, h).start()

        @pl.when(h >= 1)
        def _():
            relay(1, h - 1)

    lag = 2 + 3 * (top - y)

    @pl.loop(0, heads + 2 + 3 * top)
    def _(step):
        @pl.when(step < heads)
        def _():
            forward(step)

        @pl.when(step >= 1)
        def _():
            @pl.when(step <= heads)
            def _():
                relay(0, step - 1)

        @pl.when(step >= lag)
        def _():
            @pl.when(step < lag + heads)
            def _():
                backward(step - lag)

    relay(1, heads - 1)

    for which in range(2):
        for side in range(2):
            block[side, sent[which], which] = summed[which, side, sent[which]]

        @pl.loop(2, heads)
        def _(h):
            z_copy(which, h).wait_recv()
            block[h % 2, sent[which], which] += rz[which, h, sent[which]]

    for side in range(2):
        block[side, tiles, 1] = jnp.zeros((8, HEAD), jnp.float32)
    low_copy = exchange(block.at[1 - low], rlo, slo, klo, to_low)
    low_copy.start()
    low_copy.wait_recv()
    slim[...] = block[low] + rlo[...]

    def row_copy(k):
        return exchange(slim.at[(y + k) % rows], rrow.at[k, pl.ds(0, 2)], srow.at[k], krow.at[k], to_y(k))

    def gain_copy(k):
        return exchange(slim.at[tiles, pl.ds(0, 1)], rrow.at[k, pl.ds(2, 1)], srowg.at[k], krowg.at[k], to_y(k))

    @pl.loop(1, rows)
    def _(k):
        row_copy(k).start()
        gain_copy(k).start()

    mine[pl.ds(0, 2)] = slim[y]
    mine[pl.ds(2, 1)] = slim[tiles, pl.ds(0, 1)]

    @pl.loop(1, rows)
    def _(k):
        row_copy(k).wait_recv()
        gain_copy(k).wait_recv()
        mine[...] += rrow[k]

    half_copy = exchange(mine, rhi, shi, khi, partner)
    half_copy.start()
    half_copy.wait()
    mine[...] += rhi[...]

    def gather_copy(k, at):
        return exchange(mine.at[pl.ds(0, 2)], full.at[at], sg.at[k], kg.at[k], to_y(k))

    @pl.loop(1, rows)
    def _(k):
        gather_copy(k, y).start()

    out[y] = mine[pl.ds(0, 2)]
    out[tiles, pl.ds(0, 1)] = mine[pl.ds(2, 1)]
    out[tiles, 1] = jnp.zeros((8, HEAD), jnp.float32)

    @pl.loop(1, rows)
    def _(k):
        at = (y + rows - k) % rows
        gather_copy(k, at).wait_recv()
        out[at] = full[at]

    low_copy.wait_send()

    @pl.loop(1, rows)
    def _(k):
        row_copy(k).wait_send()
        gain_copy(k).wait_send()
        gather_copy(k, y).wait_send()

    for which in range(2):
        @pl.loop(0, heads)
        def _(h):
            core_copy(which, h).wait_send()

            @pl.when(h >= 2)
            def _():
                z_copy(which, h).wait_send()

    @pl.loop(0, heads)
    def _(h):
        across(h).wait_send()
        across_adj(h).wait_send()

        @pl.when(y != top)
        def _():
            upward(h).wait_send()

        @pl.when(y != 0)
        def _():
            downward(h).wait_send()


def attention(query, key, value, cotangent, wq, wk, gain, depth, rows):
    heads = wq.shape[0] // HEAD
    tokens, width = query.shape
    tiles = HEAD // 16
    states = pltpu.VMEM((heads, HEAD, HEAD), jnp.float32)
    dma = pltpu.SemaphoreType.DMA((heads,))
    one, each = pltpu.SemaphoreType.DMA, pltpu.SemaphoreType.DMA((rows,))

    def f32(*shape):
        return pltpu.VMEM(shape + (8, HEAD), jnp.float32)

    vmem = pl.BlockSpec(memory_space=pltpu.VMEM)
    grads = jax.ShapeDtypeStruct((tokens, width), jnp.bfloat16)
    return pl.pallas_call(
        functools.partial(attention_kernel, depth, rows),
        out_shape=(grads, grads, grads,
                   jax.ShapeDtypeStruct((tiles + 1, 2, 8, HEAD), jnp.float32)),
        in_specs=[vmem] * 7,
        out_specs=(vmem,) * 4,
        scratch_shapes=[states] * 8
        + [pltpu.VMEM((heads, tokens, HEAD), jnp.bfloat16), pltpu.VMEM((heads, tokens, HEAD), jnp.float32)]
        + [pltpu.VMEM((heads, tokens, HEAD), jnp.float32)] * 2
        + [f32(2, 2, heads, tiles + 1), f32(2, heads, tiles + 1), f32(2, heads, tiles + 1), f32(2, heads, tiles + 1)]
        + [f32(2, tiles + 1, 2), f32(tiles + 1, 2), f32(tiles + 1, 2), f32(rows, 3), f32(3), f32(3), f32(rows, 2)]
        + [dma] * 8
        + [pltpu.SemaphoreType.DMA((2, heads))] * 4
        + [one, one, each, each, each, each, one, one, each, each],
        compiler_params=pltpu.CompilerParams(collective_id=0, has_side_effects=True),
        name="attention",
    )(query, key, value, cotangent, wq, wk, gain)


def per_device(depth, rows, query_in, key_in, value_in, grad_out, w_query, w_key, norm_gain):
    width_all = query_in.shape[2]
    grad_query, grad_key, grad_value, total = attention(
        query_in[0], key_in[0], value_in[0], grad_out[0], w_query, w_key, norm_gain.reshape(1, width_all), depth, rows)
    own = HEAD // 2
    pairs = total[:-1]
    gains = total[-1, 0, 0].reshape(2, own)
    total_gain = jnp.where(lax.axis_index("dp") % 2 == 0, gains[0], gains[1])
    return (
        grad_query[None],
        grad_key[None],
        grad_value[None],
        pairs[:, 0].reshape(own, HEAD),
        pairs[:, 1].reshape(own, HEAD),
        total_gain,
    )


def solution(mesh):
    tokens = P("dp", "seq", None)
    body = functools.partial(per_device, mesh.shape["dp"] // 4, mesh.shape["seq"] // 2)
    return jax.shard_map(
        body,
        mesh=mesh,
        in_specs=(tokens, tokens, tokens, tokens, P(), P(), P()),
        out_specs=(tokens, tokens, tokens, P("dp", None), P("dp", None), P("dp")),
        check_vma=False,
    )
```

```python
import functools

import jax
import jax.numpy as jnp
from jax import lax
from jax.experimental import pallas as pl
from jax.experimental.pallas import tpu as pltpu
from jax.sharding import PartitionSpec as P

HEAD = 128
MESH = pl.DeviceIdType.MESH

norm_eps = 1e-05


def product(left, right, over):
    return lax.dot_general(left, right, ((over[:1], over[1:]), ((), ())), preferred_element_type=jnp.float32)


def two_terms(wide):
    high = wide.astype(jnp.bfloat16)
    return high, (wide - high.astype(jnp.float32)).astype(jnp.bfloat16)


def exchange(src, dst, send_sem, recv_sem, device):
    return pltpu.make_async_remote_copy(
        src_ref=src, dst_ref=dst, send_sem=send_sem, recv_sem=recv_sem, device_id=device, device_id_type=MESH)


def attention_kernel(depth, rows, query, key, value, cotangent, wq, wk, gain, grad_query, grad_key, grad_value, out,
                     local, peer, inbox, outbox, adjoint, peer_adj, inbox_adj, outbox_adj,
                     feat_k, slope_k, part_fk, part_v, parts, rcore, summed, rz, block, rlo, slim, rrow, mine, rhi, full,
                     sx, rx, sy, ry, sx2, rx2, sy2, ry2, score, kcore, sz, kz,
                     slo, klo, srow, krow, srowg, krowg, shi, khi, sg, kg):
    heads = local.shape[0]
    dp, seq = lax.axis_index("dp"), lax.axis_index("seq")
    y, half = seq // 2, seq % 2
    top = rows - 1
    z, low, core = dp // 4, (dp // 2) % 2, dp % 2

    def to_z(k):
        return (((z + k) % depth) * 4 + low * 2 + core, seq)

    def to_y(k):
        return (dp, ((y + k) % rows) * 2 + half)

    to_core = (z * 4 + low * 2 + (1 - core), seq)
    to_low = (z * 4 + (1 - low) * 2 + core, seq)
    partner = (dp, y * 2 + (1 - half))
    above, below = to_y(1), to_y(rows - 1)
    barrier = pltpu.get_barrier_semaphore()
    others = [to_core, to_low, partner]
    others += [to_z(k) for k in range(1, depth)] + [to_y(k) for k in range(1, rows)]
    for other in others:
        pl.semaphore_signal(barrier, inc=1, device_id=other, device_id_type=MESH)
    pl.semaphore_wait(barrier, len(others))

    def across(h):
        return exchange(local.at[h], peer.at[h], sx.at[h], rx.at[h], partner)

    def upward(h):
        return exchange(outbox.at[h], inbox.at[h], sy.at[h], ry.at[h], above)

    def across_adj(h):
        return exchange(adjoint.at[h], peer_adj.at[h], sx2.at[h], rx2.at[h], partner)

    def downward(h):
        return exchange(outbox_adj.at[h], inbox_adj.at[h], sy2.at[h], ry2.at[h], below)

    def columns(h):
        return pl.ds(pl.multiple_of(((h + 2 * z) % heads) * HEAD, HEAD), HEAD)

    tiles = HEAD // 16
    sent = (pl.ds(0, tiles + 1), pl.ds(0, tiles))

    def core_copy(which, h):
        return exchange(parts.at[which, 1 - core, h, sent[which]], rcore.at[which, h, sent[which]],
                        score.at[which, h], kcore.at[which, h], to_core)

    def z_copy(which, h):
        return exchange(summed.at[which, h, sent[which]], rz.at[which, h, sent[which]],
                        sz.at[which, h], kz.at[which, h], to_z(h // 2))

    def relay(which, h):
        core_copy(which, h).wait_recv()
        summed[which, h, sent[which]] = parts[which, core, h, sent[which]] + rcore[which, h, sent[which]]

        @pl.when(h >= 2)
        def _():
            z_copy(which, h).start()

    tokens = query.shape[0]
    position = lax.broadcasted_iota(jnp.int32, (tokens, tokens), 0)
    column = lax.broadcasted_iota(jnp.int32, (tokens, tokens), 1)
    causal = position >= column

    def put_sums(h, which, total):
        own = HEAD // 2
        for side in range(2):
            parts[which, side, h, pl.ds(0, tiles)] = total[side * own : (side + 1) * own].reshape(tiles, 8, HEAD)

    @pl.loop(0, heads)
    def _(h):
        at = columns(h)
        pre = product(key[:, at], wk[at, :], (1, 0))
        slope = jnp.exp(jnp.minimum(pre, 0.0))
        feat = jnp.where(pre > 0.0, pre + 1.0, slope).astype(jnp.bfloat16)
        slope_k[h] = slope
        feat_k[h] = feat
        local[h] = product(feat, value[:, at], (0, 0))

        @pl.when(h > 0)
        def _():
            across(h - 1).start()

    @pl.when(y == 0)
    def _():
        inbox[...] = jnp.zeros_like(inbox)

    @pl.when(y == top)
    def _():
        inbox_adj[...] = jnp.zeros_like(inbox_adj)

    across(heads - 1).start()
    is_second = jnp.where(half == 1, 1.0, 0.0).astype(jnp.float32)

    def forward(h):
        at = columns(h)
        fk, v = feat_k[h], value[:, at]
        q, wq_h = query[:, at], wq[at, :]
        pre = product(q, wq_h, (1, 0))
        slope = jnp.exp(jnp.minimum(pre, 0.0))
        fq = jnp.where(pre > 0.0, pre + 1.0, slope).astype(jnp.bfloat16)
        attn = jnp.where(causal, product(fq, fk, (1, 1)), 0.0).astype(jnp.bfloat16)
        inner = product(attn, v, (1, 0))
        across(h).wait_recv()

        @pl.when(y != 0)
        def _():
            upward(h).wait_recv()

        outbox[h] = inbox[h] + (local[h] + peer[h])
        state_high, state_low = two_terms(inbox[h] + is_second * peer[h])

        @pl.when(y != top)
        def _():
            upward(h).start()

        numerator = inner + (product(fq, state_high, (1, 0)) + product(fq, state_low, (1, 0)))
        inv_rms = lax.rsqrt(jnp.mean(numerator * numerator, axis=-1, keepdims=True) + norm_eps)
        normed = numerator * inv_rms
        grad = cotangent[:, at].astype(jnp.float32)
        grad_normed = grad * gain[:, at]
        grad_numer = inv_rms * (
            grad_normed - normed * jnp.mean(grad_normed * normed, axis=-1, keepdims=True))
        low_numer, rest = two_terms(grad_numer)
        adjoint[h] = product(fq, low_numer, (0, 0))
        mixed = jnp.where(causal, product(low_numer, v, (1, 1)), 0.0).astype(jnp.bfloat16)
        grad_fq = product(mixed, fk, (1, 0)) + (
            product(low_numer, state_high, (1, 1)) + (product(low_numer, state_low, (1, 1)) + product(rest, state_high, (1, 1))))
        across_adj(h).start()
        pre_grad = (grad_fq * slope).astype(jnp.bfloat16)
        grad_query[:, at] = product(pre_grad, wq_h, (1, 1)).astype(jnp.bfloat16)
        put_sums(h, 0, product(q, pre_grad, (0, 0)))
        gains = jnp.broadcast_to(jnp.sum(normed * grad, axis=0, keepdims=True), (8, HEAD))
        for side in range(2):
            parts[0, side, h, tiles] = gains
        part_fk[h] = product(mixed, fq, (0, 0))
        part_v[h] = product(attn, low_numer, (0, 0))
        core_copy(0, h).start()

    def backward(h):
        at = columns(h)
        across_adj(h).wait_recv()

        @pl.when(y != top)
        def _():
            downward(h).wait_recv()

        outbox_adj[h] = inbox_adj[h] + (adjoint[h] + peer_adj[h])
        state_high, state_low = two_terms(inbox_adj[h] + (1.0 - is_second) * peer_adj[h])

        @pl.when(y != 0)
        def _():
            downward(h).start()

        v, fk, wk_h = value[:, at], feat_k[h], wk[at, :]
        grad_fk = part_fk[h] + (product(v, state_high, (1, 1)) + product(v, state_low, (1, 1)))
        pre_grad = (grad_fk * slope_k[h]).astype(jnp.bfloat16)
        grad_v = part_v[h] + (product(fk, state_high, (1, 0)) + product(fk, state_low, (1, 0)))
        put_sums(h, 1, product(key[:, at], pre_grad, (0, 0)))
        grad_value[:, at] = grad_v.astype(jnp.bfloat16)
        grad_key[:, at] = product(pre_grad, wk_h, (1, 1)).astype(jnp.bfloat16)
        core_copy(1, h).start()

        @pl.when(h >= 2)
        def _():
            relay(1, h - 2)

    lag = 3 + 6 * (top - y)

    @pl.loop(0, heads + 3 + 6 * top)
    def _(step):
        @pl.when(step < heads)
        def _():
            forward(step)

        @pl.when(step >= 3)
        def _():
            @pl.when(step < heads + 3)
            def _():
                relay(0, step - 3)

        @pl.when(step >= lag)
        def _():
            @pl.when(step < lag + heads)
            def _():
                backward(step - lag)

    relay(1, heads - 2)
    relay(1, heads - 1)

    for which in range(2):
        for side in range(2):
            block[side, sent[which], which] = summed[which, side, sent[which]]

        @pl.loop(2, heads)
        def _(h):
            z_copy(which, h).wait_recv()
            block[h % 2, sent[which], which] += rz[which, h, sent[which]]

    for side in range(2):
        block[side, tiles, 1] = jnp.zeros((8, HEAD), jnp.float32)
    low_copy = exchange(block.at[1 - low], rlo, slo, klo, to_low)
    low_copy.start()
    low_copy.wait_recv()
    slim[...] = block[low] + rlo[...]

    def row_copy(k):
        return exchange(slim.at[(y + k) % rows], rrow.at[k, pl.ds(0, 2)], srow.at[k], krow.at[k], to_y(k))

    def gain_copy(k):
        return exchange(slim.at[tiles, pl.ds(0, 1)], rrow.at[k, pl.ds(2, 1)], srowg.at[k], krowg.at[k], to_y(k))

    @pl.loop(1, rows)
    def _(k):
        row_copy(k).start()
        gain_copy(k).start()

    mine[pl.ds(0, 2)] = slim[y]
    mine[pl.ds(2, 1)] = slim[tiles, pl.ds(0, 1)]

    @pl.loop(1, rows)
    def _(k):
        row_copy(k).wait_recv()
        gain_copy(k).wait_recv()
        mine[...] += rrow[k]

    half_copy = exchange(mine, rhi, shi, khi, partner)
    half_copy.start()
    half_copy.wait()
    mine[...] += rhi[...]

    def gather_copy(k, at):
        return exchange(mine.at[pl.ds(0, 2)], full.at[at], sg.at[k], kg.at[k], to_y(k))

    @pl.loop(1, rows)
    def _(k):
        gather_copy(k, y).start()

    out[y] = mine[pl.ds(0, 2)]
    out[tiles, pl.ds(0, 1)] = mine[pl.ds(2, 1)]
    out[tiles, 1] = jnp.zeros((8, HEAD), jnp.float32)

    @pl.loop(1, rows)
    def _(k):
        at = (y + rows - k) % rows
        gather_copy(k, at).wait_recv()
        out[at] = full[at]

    low_copy.wait_send()

    @pl.loop(1, rows)
    def _(k):
        row_copy(k).wait_send()
        gain_copy(k).wait_send()
        gather_copy(k, y).wait_send()

    for which in range(2):
        @pl.loop(0, heads)
        def _(h):
            core_copy(which, h).wait_send()

            @pl.when(h >= 2)
            def _():
                z_copy(which, h).wait_send()

    @pl.loop(0, heads)
    def _(h):
        across(h).wait_send()
        across_adj(h).wait_send()

        @pl.when(y != top)
        def _():
            upward(h).wait_send()

        @pl.when(y != 0)
        def _():
            downward(h).wait_send()


def attention(query, key, value, cotangent, wq, wk, gain, depth, rows):
    heads = wq.shape[0] // HEAD
    tokens, width = query.shape
    tiles = HEAD // 16
    states = pltpu.VMEM((heads, HEAD, HEAD), jnp.float32)
    dma = pltpu.SemaphoreType.DMA((heads,))
    one, each = pltpu.SemaphoreType.DMA, pltpu.SemaphoreType.DMA((rows,))

    def f32(*shape):
        return pltpu.VMEM(shape + (8, HEAD), jnp.float32)

    vmem = pl.BlockSpec(memory_space=pltpu.VMEM)
    grads = jax.ShapeDtypeStruct((tokens, width), jnp.bfloat16)
    return pl.pallas_call(
        functools.partial(attention_kernel, depth, rows),
        out_shape=(grads, grads, grads,
                   jax.ShapeDtypeStruct((tiles + 1, 2, 8, HEAD), jnp.float32)),
        in_specs=[vmem] * 7,
        out_specs=(vmem,) * 4,
        scratch_shapes=[states] * 8
        + [pltpu.VMEM((heads, tokens, HEAD), jnp.bfloat16), pltpu.VMEM((heads, tokens, HEAD), jnp.float32)]
        + [pltpu.VMEM((heads, tokens, HEAD), jnp.float32)] * 2
        + [f32(2, 2, heads, tiles + 1), f32(2, heads, tiles + 1), f32(2, heads, tiles + 1), f32(2, heads, tiles + 1)]
        + [f32(2, tiles + 1, 2), f32(tiles + 1, 2), f32(tiles + 1, 2), f32(rows, 3), f32(3), f32(3), f32(rows, 2)]
        + [dma] * 8
        + [pltpu.SemaphoreType.DMA((2, heads))] * 4
        + [one, one, each, each, each, each, one, one, each, each],
        compiler_params=pltpu.CompilerParams(collective_id=0, has_side_effects=True),
        name="attention",
    )(query, key, value, cotangent, wq, wk, gain)


def per_device(depth, rows, query_in, key_in, value_in, grad_out, w_query, w_key, norm_gain):
    width_all = query_in.shape[2]
    grad_query, grad_key, grad_value, total = attention(
        query_in[0], key_in[0], value_in[0], grad_out[0], w_query, w_key, norm_gain.reshape(1, width_all), depth, rows)
    own = HEAD // 2
    pairs = total[:-1]
    gains = total[-1, 0, 0].reshape(2, own)
    total_gain = jnp.where(lax.axis_index("dp") % 2 == 0, gains[0], gains[1])
    return (
        grad_query[None],
        grad_key[None],
        grad_value[None],
        pairs[:, 0].reshape(own, HEAD),
        pairs[:, 1].reshape(own, HEAD),
        total_gain,
    )


def solution(mesh):
    tokens = P("dp", "seq", None)
    body = functools.partial(per_device, mesh.shape["dp"] // 4, mesh.shape["seq"] // 2)
    return jax.shard_map(
        body,
        mesh=mesh,
        in_specs=(tokens, tokens, tokens, tokens, P(), P(), P()),
        out_specs=(tokens, tokens, tokens, P("dp", None), P("dp", None), P("dp")),
        check_vma=False,
    )
```

```python
import functools

import jax
import jax.numpy as jnp
from jax import lax
from jax.experimental import pallas as pl
from jax.experimental.pallas import tpu as pltpu
from jax.sharding import PartitionSpec as P

HEAD = 128
PIECES = 4
MESH = pl.DeviceIdType.MESH

norm_eps = 1e-05


def product(left, right, over):
    return lax.dot_general(left, right, ((over[:1], over[1:]), ((), ())), preferred_element_type=jnp.float32)


def two_terms(wide):
    high = wide.astype(jnp.bfloat16)
    return high, (wide - high.astype(jnp.float32)).astype(jnp.bfloat16)


def exchange(src, dst, send_sem, recv_sem, device):
    return pltpu.make_async_remote_copy(
        src_ref=src, dst_ref=dst, send_sem=send_sem, recv_sem=recv_sem, device_id=device, device_id_type=MESH)


def attention_kernel(depth, rows, query, key, value, cotangent, wq, wk, gain, grad_query, grad_key, grad_value, out,
                     local, peer, inbox, outbox, adjoint, peer_adj, inbox_adj, outbox_adj,
                     feat_k, slope_k, part_fk, part_v, parts, rcore, summed, rz, block, rlo, slim, rrow, mine, rhi, full,
                     sx, rx, sy, ry, sx2, rx2, sy2, ry2, score, kcore, sz, kz,
                     slo, klo, srow, krow, srowg, krowg, shi, khi, sg, kg):
    heads = local.shape[0]
    dp, seq = lax.axis_index("dp"), lax.axis_index("seq")
    y, half = seq // 2, seq % 2
    top = rows - 1
    z, low, core = dp // 4, (dp // 2) % 2, dp % 2

    def to_z(k):
        return (((z + k) % depth) * 4 + low * 2 + core, seq)

    def to_y(k):
        return (dp, ((y + k) % rows) * 2 + half)

    to_core = (z * 4 + low * 2 + (1 - core), seq)
    to_low = (z * 4 + (1 - low) * 2 + core, seq)
    partner = (dp, y * 2 + (1 - half))
    above, below = to_y(1), to_y(rows - 1)
    barrier = pltpu.get_barrier_semaphore()
    others = [to_core, to_low, partner]
    others += [to_z(k) for k in range(1, depth)] + [to_y(k) for k in range(1, rows)]
    for other in others:
        pl.semaphore_signal(barrier, inc=1, device_id=other, device_id_type=MESH)
    pl.semaphore_wait(barrier, len(others))

    def across(h):
        return exchange(local.at[h], peer.at[h], sx.at[h], rx.at[h], partner)

    def piece(p):
        return pl.ds(p * (HEAD // PIECES), HEAD // PIECES)

    def upward(h, p):
        return exchange(outbox.at[h, piece(p)], inbox.at[h, piece(p)], sy.at[h, p], ry.at[h, p], above)

    def across_adj(h):
        return exchange(adjoint.at[h], peer_adj.at[h], sx2.at[h], rx2.at[h], partner)

    def downward(h, p):
        return exchange(outbox_adj.at[h, piece(p)], inbox_adj.at[h, piece(p)], sy2.at[h, p], ry2.at[h, p], below)

    def joined(terms):
        return tuple(jnp.concatenate(parts_of, axis=0) for parts_of in zip(*terms))

    def columns(h):
        return pl.ds(pl.multiple_of(((h + 2 * z) % heads) * HEAD, HEAD), HEAD)

    tiles = HEAD // 16
    sent = (pl.ds(0, tiles + 1), pl.ds(0, tiles))

    def core_copy(which, h):
        return exchange(parts.at[which, 1 - core, h, sent[which]], rcore.at[which, h, sent[which]],
                        score.at[which, h], kcore.at[which, h], to_core)

    def z_copy(which, h):
        return exchange(summed.at[which, h, sent[which]], rz.at[which, h, sent[which]],
                        sz.at[which, h], kz.at[which, h], to_z(h // 2))

    def relay(which, h):
        core_copy(which, h).wait_recv()
        summed[which, h, sent[which]] = parts[which, core, h, sent[which]] + rcore[which, h, sent[which]]

        @pl.when(h >= 2)
        def _():
            z_copy(which, h).start()

    tokens = query.shape[0]
    position = lax.broadcasted_iota(jnp.int32, (tokens, tokens), 0)
    column = lax.broadcasted_iota(jnp.int32, (tokens, tokens), 1)
    causal = position >= column

    def put_sums(h, which, total):
        own = HEAD // 2
        for side in range(2):
            parts[which, side, h, pl.ds(0, tiles)] = total[side * own : (side + 1) * own].reshape(tiles, 8, HEAD)

    @pl.loop(0, heads)
    def _(h):
        at = columns(h)
        pre = product(key[:, at], wk[at, :], (1, 0))
        slope = jnp.exp(jnp.minimum(pre, 0.0))
        feat = jnp.where(pre > 0.0, pre + 1.0, slope).astype(jnp.bfloat16)
        slope_k[h] = slope
        feat_k[h] = feat
        local[h] = product(feat, value[:, at], (0, 0))

        @pl.when(h > 0)
        def _():
            across(h - 1).start()

    @pl.when(y == 0)
    def _():
        inbox[...] = jnp.zeros_like(inbox)

    @pl.when(y == top)
    def _():
        inbox_adj[...] = jnp.zeros_like(inbox_adj)

    across(heads - 1).start()
    is_second = jnp.where(half == 1, 1.0, 0.0).astype(jnp.float32)

    def forward(h):
        at = columns(h)
        fk, v = feat_k[h], value[:, at]
        q, wq_h = query[:, at], wq[at, :]
        pre = product(q, wq_h, (1, 0))
        slope = jnp.exp(jnp.minimum(pre, 0.0))
        fq = jnp.where(pre > 0.0, pre + 1.0, slope).astype(jnp.bfloat16)
        attn = jnp.where(causal, product(fq, fk, (1, 1)), 0.0).astype(jnp.bfloat16)
        inner = product(attn, v, (1, 0))
        across(h).wait_recv()

        terms = []
        for p in range(PIECES):
            @pl.when(y != 0)
            def _():
                upward(h, p).wait_recv()

            some = piece(p)
            outbox[h, some] = inbox[h, some] + (local[h, some] + peer[h, some])
            terms.append(two_terms(inbox[h, some] + is_second * peer[h, some]))

            @pl.when(y != top)
            def _():
                upward(h, p).start()

        state_high, state_low = joined(terms)

        numerator = inner + (product(fq, state_high, (1, 0)) + product(fq, state_low, (1, 0)))
        inv_rms = lax.rsqrt(jnp.mean(numerator * numerator, axis=-1, keepdims=True) + norm_eps)
        normed = numerator * inv_rms
        grad = cotangent[:, at].astype(jnp.float32)
        grad_normed = grad * gain[:, at]
        grad_numer = inv_rms * (
            grad_normed - normed * jnp.mean(grad_normed * normed, axis=-1, keepdims=True))
        low_numer, rest = two_terms(grad_numer)
        adjoint[h] = product(fq, low_numer, (0, 0))
        mixed = jnp.where(causal, product(low_numer, v, (1, 1)), 0.0).astype(jnp.bfloat16)
        grad_fq = product(mixed, fk, (1, 0)) + (
            product(low_numer, state_high, (1, 1)) + (product(low_numer, state_low, (1, 1)) + product(rest, state_high, (1, 1))))
        across_adj(h).start()
        pre_grad = (grad_fq * slope).astype(jnp.bfloat16)
        grad_query[:, at] = product(pre_grad, wq_h, (1, 1)).astype(jnp.bfloat16)
        put_sums(h, 0, product(q, pre_grad, (0, 0)))
        gains = jnp.broadcast_to(jnp.sum(normed * grad, axis=0, keepdims=True), (8, HEAD))
        for side in range(2):
            parts[0, side, h, tiles] = gains
        part_fk[h] = product(mixed, fq, (0, 0))
        part_v[h] = product(attn, low_numer, (0, 0))
        core_copy(0, h).start()

    def backward(h):
        at = columns(h)
        across_adj(h).wait_recv()

        terms = []
        for p in range(PIECES):
            @pl.when(y != top)
            def _():
                downward(h, p).wait_recv()

            some = piece(p)
            outbox_adj[h, some] = inbox_adj[h, some] + (adjoint[h, some] + peer_adj[h, some])
            terms.append(two_terms(inbox_adj[h, some] + (1.0 - is_second) * peer_adj[h, some]))

            @pl.when(y != 0)
            def _():
                downward(h, p).start()

        state_high, state_low = joined(terms)

        v, fk, wk_h = value[:, at], feat_k[h], wk[at, :]
        grad_fk = part_fk[h] + (product(v, state_high, (1, 1)) + product(v, state_low, (1, 1)))
        pre_grad = (grad_fk * slope_k[h]).astype(jnp.bfloat16)
        grad_v = part_v[h] + (product(fk, state_high, (1, 0)) + product(fk, state_low, (1, 0)))
        put_sums(h, 1, product(key[:, at], pre_grad, (0, 0)))
        grad_value[:, at] = grad_v.astype(jnp.bfloat16)
        grad_key[:, at] = product(pre_grad, wk_h, (1, 1)).astype(jnp.bfloat16)
        core_copy(1, h).start()

        @pl.when(h >= 2)
        def _():
            relay(1, h - 2)

    lag = 3 + 6 * (top - y)

    @pl.loop(0, heads + 3 + 6 * top)
    def _(step):
        @pl.when(step < heads)
        def _():
            forward(step)

        @pl.when(step >= 3)
        def _():
            @pl.when(step < heads + 3)
            def _():
                relay(0, step - 3)

        @pl.when(step >= lag)
        def _():
            @pl.when(step < lag + heads)
            def _():
                backward(step - lag)

    relay(1, heads - 2)
    relay(1, heads - 1)

    for which in range(2):
        for side in range(2):
            block[side, sent[which], which] = summed[which, side, sent[which]]

        @pl.loop(2, heads)
        def _(h):
            z_copy(which, h).wait_recv()
            block[h % 2, sent[which], which] += rz[which, h, sent[which]]

    for side in range(2):
        block[side, tiles, 1] = jnp.zeros((8, HEAD), jnp.float32)
    low_copy = exchange(block.at[1 - low], rlo, slo, klo, to_low)
    low_copy.start()
    low_copy.wait_recv()
    slim[...] = block[low] + rlo[...]

    def row_copy(k):
        return exchange(slim.at[(y + k) % rows], rrow.at[k, pl.ds(0, 2)], srow.at[k], krow.at[k], to_y(k))

    def gain_copy(k):
        return exchange(slim.at[tiles, pl.ds(0, 1)], rrow.at[k, pl.ds(2, 1)], srowg.at[k], krowg.at[k], to_y(k))

    @pl.loop(1, rows)
    def _(k):
        row_copy(k).start()
        gain_copy(k).start()

    mine[pl.ds(0, 2)] = slim[y]
    mine[pl.ds(2, 1)] = slim[tiles, pl.ds(0, 1)]

    @pl.loop(1, rows)
    def _(k):
        row_copy(k).wait_recv()
        gain_copy(k).wait_recv()
        mine[...] += rrow[k]

    half_copy = exchange(mine, rhi, shi, khi, partner)
    half_copy.start()
    half_copy.wait()
    mine[...] += rhi[...]

    def gather_copy(k, at):
        return exchange(mine.at[pl.ds(0, 2)], full.at[at], sg.at[k], kg.at[k], to_y(k))

    @pl.loop(1, rows)
    def _(k):
        gather_copy(k, y).start()

    out[y] = mine[pl.ds(0, 2)]
    out[tiles, pl.ds(0, 1)] = mine[pl.ds(2, 1)]
    out[tiles, 1] = jnp.zeros((8, HEAD), jnp.float32)

    @pl.loop(1, rows)
    def _(k):
        at = (y + rows - k) % rows
        gather_copy(k, at).wait_recv()
        out[at] = full[at]

    low_copy.wait_send()

    @pl.loop(1, rows)
    def _(k):
        row_copy(k).wait_send()
        gain_copy(k).wait_send()
        gather_copy(k, y).wait_send()

    for which in range(2):
        @pl.loop(0, heads)
        def _(h):
            core_copy(which, h).wait_send()

            @pl.when(h >= 2)
            def _():
                z_copy(which, h).wait_send()

    @pl.loop(0, heads)
    def _(h):
        across(h).wait_send()
        across_adj(h).wait_send()

        for p in range(PIECES):
            @pl.when(y != top)
            def _():
                upward(h, p).wait_send()

            @pl.when(y != 0)
            def _():
                downward(h, p).wait_send()


def attention(query, key, value, cotangent, wq, wk, gain, depth, rows):
    heads = wq.shape[0] // HEAD
    tokens, width = query.shape
    tiles = HEAD // 16
    states = pltpu.VMEM((heads, HEAD, HEAD), jnp.float32)
    dma, pieces = pltpu.SemaphoreType.DMA((heads,)), pltpu.SemaphoreType.DMA((heads, PIECES))
    one, each = pltpu.SemaphoreType.DMA, pltpu.SemaphoreType.DMA((rows,))

    def f32(*shape):
        return pltpu.VMEM(shape + (8, HEAD), jnp.float32)

    vmem = pl.BlockSpec(memory_space=pltpu.VMEM)
    grads = jax.ShapeDtypeStruct((tokens, width), jnp.bfloat16)
    return pl.pallas_call(
        functools.partial(attention_kernel, depth, rows),
        out_shape=(grads, grads, grads,
                   jax.ShapeDtypeStruct((tiles + 1, 2, 8, HEAD), jnp.float32)),
        in_specs=[vmem] * 7,
        out_specs=(vmem,) * 4,
        scratch_shapes=[states] * 8
        + [pltpu.VMEM((heads, tokens, HEAD), jnp.bfloat16), pltpu.VMEM((heads, tokens, HEAD), jnp.float32)]
        + [pltpu.VMEM((heads, tokens, HEAD), jnp.float32)] * 2
        + [f32(2, 2, heads, tiles + 1), f32(2, heads, tiles + 1), f32(2, heads, tiles + 1), f32(2, heads, tiles + 1)]
        + [f32(2, tiles + 1, 2), f32(tiles + 1, 2), f32(tiles + 1, 2), f32(rows, 3), f32(3), f32(3), f32(rows, 2)]
        + [dma, dma, pieces, pieces] * 2
        + [pltpu.SemaphoreType.DMA((2, heads))] * 4
        + [one, one, each, each, each, each, one, one, each, each],
        compiler_params=pltpu.CompilerParams(collective_id=0, has_side_effects=True),
        name="attention",
    )(query, key, value, cotangent, wq, wk, gain)


def per_device(depth, rows, query_in, key_in, value_in, grad_out, w_query, w_key, norm_gain):
    width_all = query_in.shape[2]
    grad_query, grad_key, grad_value, total = attention(
        query_in[0], key_in[0], value_in[0], grad_out[0], w_query, w_key, norm_gain.reshape(1, width_all), depth, rows)
    own = HEAD // 2
    pairs = total[:-1]
    gains = total[-1, 0, 0].reshape(2, own)
    total_gain = jnp.where(lax.axis_index("dp") % 2 == 0, gains[0], gains[1])
    return (
        grad_query[None],
        grad_key[None],
        grad_value[None],
        pairs[:, 0].reshape(own, HEAD),
        pairs[:, 1].reshape(own, HEAD),
        total_gain,
    )


def solution(mesh):
    tokens = P("dp", "seq", None)
    body = functools.partial(per_device, mesh.shape["dp"] // 4, mesh.shape["seq"] // 2)
    return jax.shard_map(
        body,
        mesh=mesh,
        in_specs=(tokens, tokens, tokens, tokens, P(), P(), P()),
        out_specs=(tokens, tokens, tokens, P("dp", None), P("dp", None), P("dp")),
        check_vma=False,
    )
```

```python
import functools

import jax
import jax.numpy as jnp
from jax import lax
from jax.experimental import pallas as pl
from jax.experimental.pallas import tpu as pltpu
from jax.sharding import PartitionSpec as P

HEAD = 128
PIECES = 4
MESH = pl.DeviceIdType.MESH

norm_eps = 1e-05


def product(left, right, over):
    return lax.dot_general(left, right, ((over[:1], over[1:]), ((), ())), preferred_element_type=jnp.float32)


def two_terms(wide):
    high = wide.astype(jnp.bfloat16)
    return high, (wide - high.astype(jnp.float32)).astype(jnp.bfloat16)


def exchange(src, dst, send_sem, recv_sem, device):
    return pltpu.make_async_remote_copy(
        src_ref=src, dst_ref=dst, send_sem=send_sem, recv_sem=recv_sem, device_id=device, device_id_type=MESH)


def attention_kernel(depth, rows, query, key, value, cotangent, wq, wk, gain, grad_query, grad_key, grad_value, out_wq, out_wk, out_gain,
                     local, peer, inbox, outbox, adjoint, peer_adj, inbox_adj, outbox_adj,
                     feat_k, slope_k, part_fk, part_v, parts, rcore, summed, rz, block, rlo, slim, rrow, mine, rhi, full,
                     sx, rx, sy, ry, sx2, rx2, sy2, ry2, score, kcore, sz, kz,
                     slo, klo, srow, krow, srowg, krowg, shi, khi, sg, kg):
    heads = local.shape[0]
    dp, seq = lax.axis_index("dp"), lax.axis_index("seq")
    y, half = seq // 2, seq % 2
    top = rows - 1
    z, low, core = dp // 4, (dp // 2) % 2, dp % 2

    def to_z(k):
        return (((z + k) % depth) * 4 + low * 2 + core, seq)

    def to_y(k):
        return (dp, ((y + k) % rows) * 2 + half)

    to_core = (z * 4 + low * 2 + (1 - core), seq)
    to_low = (z * 4 + (1 - low) * 2 + core, seq)
    partner = (dp, y * 2 + (1 - half))
    above, below = to_y(1), to_y(rows - 1)
    barrier = pltpu.get_barrier_semaphore()
    others = [to_core, to_low, partner]
    others += [to_z(k) for k in range(1, depth)] + [to_y(k) for k in range(1, rows)]
    for other in others:
        pl.semaphore_signal(barrier, inc=1, device_id=other, device_id_type=MESH)
    pl.semaphore_wait(barrier, len(others))

    def across(h):
        return exchange(local.at[h], peer.at[h], sx.at[h], rx.at[h], partner)

    def piece(p):
        return pl.ds(p * (HEAD // PIECES), HEAD // PIECES)

    def upward(h, p):
        return exchange(outbox.at[h, piece(p)], inbox.at[h, piece(p)], sy.at[h, p], ry.at[h, p], above)

    def across_adj(h):
        return exchange(adjoint.at[h], peer_adj.at[h], sx2.at[h], rx2.at[h], partner)

    def downward(h, p):
        return exchange(outbox_adj.at[h, piece(p)], inbox_adj.at[h, piece(p)], sy2.at[h, p], ry2.at[h, p], below)

    def joined(terms):
        return tuple(jnp.concatenate(parts_of, axis=0) for parts_of in zip(*terms))

    def columns(h):
        return pl.ds(pl.multiple_of(((h + 2 * z) % heads) * HEAD, HEAD), HEAD)

    tiles = HEAD // 16
    sent = (pl.ds(0, tiles + 1), pl.ds(0, tiles))

    def core_copy(which, h):
        return exchange(parts.at[which, 1 - core, h, sent[which]], rcore.at[which, h, sent[which]],
                        score.at[which, h], kcore.at[which, h], to_core)

    def z_copy(which, h):
        return exchange(summed.at[which, h, sent[which]], rz.at[which, h, sent[which]],
                        sz.at[which, h], kz.at[which, h], to_z(h // 2))

    def relay(which, h):
        core_copy(which, h).wait_recv()
        summed[which, h, sent[which]] = parts[which, core, h, sent[which]] + rcore[which, h, sent[which]]

        @pl.when(h >= 2)
        def _():
            z_copy(which, h).start()

    tokens = query.shape[0]
    position = lax.broadcasted_iota(jnp.int32, (tokens, tokens), 0)
    column = lax.broadcasted_iota(jnp.int32, (tokens, tokens), 1)
    causal = position >= column

    def put_sums(h, which, total):
        own = HEAD // 2
        for side in range(2):
            parts[which, side, h, pl.ds(0, tiles)] = total[side * own : (side + 1) * own].reshape(tiles, 8, HEAD)

    @pl.loop(0, heads)
    def _(h):
        at = columns(h)
        pre = product(key[:, at], wk[at, :], (1, 0))
        slope = jnp.exp(jnp.minimum(pre, 0.0))
        feat = jnp.where(pre > 0.0, pre + 1.0, slope).astype(jnp.bfloat16)
        slope_k[h] = slope
        feat_k[h] = feat
        local[h] = product(feat, value[:, at], (0, 0))

        @pl.when(h > 0)
        def _():
            across(h - 1).start()

    @pl.when(y == 0)
    def _():
        inbox[...] = jnp.zeros_like(inbox)

    @pl.when(y == top)
    def _():
        inbox_adj[...] = jnp.zeros_like(inbox_adj)

    across(heads - 1).start()
    is_second = jnp.where(half == 1, 1.0, 0.0).astype(jnp.float32)

    def forward(h):
        at = columns(h)
        fk, v = feat_k[h], value[:, at]
        q, wq_h = query[:, at], wq[at, :]
        pre = product(q, wq_h, (1, 0))
        slope = jnp.exp(jnp.minimum(pre, 0.0))
        fq = jnp.where(pre > 0.0, pre + 1.0, slope).astype(jnp.bfloat16)
        attn = jnp.where(causal, product(fq, fk, (1, 1)), 0.0).astype(jnp.bfloat16)
        inner = product(attn, v, (1, 0))
        across(h).wait_recv()

        terms = []
        for p in range(PIECES):
            @pl.when(y != 0)
            def _():
                upward(h, p).wait_recv()

            some = piece(p)
            outbox[h, some] = inbox[h, some] + (local[h, some] + peer[h, some])
            terms.append(two_terms(inbox[h, some] + is_second * peer[h, some]))

            @pl.when(y != top)
            def _():
                upward(h, p).start()

        state_high, state_low = joined(terms)

        numerator = inner + (product(fq, state_high, (1, 0)) + product(fq, state_low, (1, 0)))
        inv_rms = lax.rsqrt(jnp.mean(numerator * numerator, axis=-1, keepdims=True) + norm_eps)
        normed = numerator * inv_rms
        grad = cotangent[:, at].astype(jnp.float32)
        grad_normed = grad * gain[:, at]
        grad_numer = inv_rms * (
            grad_normed - normed * jnp.mean(grad_normed * normed, axis=-1, keepdims=True))
        low_numer, rest = two_terms(grad_numer)
        adjoint[h] = product(fq, low_numer, (0, 0))
        mixed = jnp.where(causal, product(low_numer, v, (1, 1)), 0.0).astype(jnp.bfloat16)
        grad_fq = product(mixed, fk, (1, 0)) + (
            product(low_numer, state_high, (1, 1)) + (product(low_numer, state_low, (1, 1)) + product(rest, state_high, (1, 1))))
        across_adj(h).start()
        pre_grad = (grad_fq * slope).astype(jnp.bfloat16)
        grad_query[:, at] = product(pre_grad, wq_h, (1, 1)).astype(jnp.bfloat16)
        put_sums(h, 0, product(q, pre_grad, (0, 0)))
        gains = jnp.broadcast_to(jnp.sum(normed * grad, axis=0, keepdims=True), (8, HEAD))
        for side in range(2):
            parts[0, side, h, tiles] = gains
        part_fk[h] = product(mixed, fq, (0, 0))
        part_v[h] = product(attn, low_numer, (0, 0))
        core_copy(0, h).start()

    def backward(h):
        at = columns(h)
        across_adj(h).wait_recv()

        terms = []
        for p in range(PIECES):
            @pl.when(y != top)
            def _():
                downward(h, p).wait_recv()

            some = piece(p)
            outbox_adj[h, some] = inbox_adj[h, some] + (adjoint[h, some] + peer_adj[h, some])
            terms.append(two_terms(inbox_adj[h, some] + (1.0 - is_second) * peer_adj[h, some]))

            @pl.when(y != 0)
            def _():
                downward(h, p).start()

        state_high, state_low = joined(terms)

        v, fk, wk_h = value[:, at], feat_k[h], wk[at, :]
        grad_fk = part_fk[h] + (product(v, state_high, (1, 1)) + product(v, state_low, (1, 1)))
        pre_grad = (grad_fk * slope_k[h]).astype(jnp.bfloat16)
        grad_v = part_v[h] + (product(fk, state_high, (1, 0)) + product(fk, state_low, (1, 0)))
        put_sums(h, 1, product(key[:, at], pre_grad, (0, 0)))
        grad_value[:, at] = grad_v.astype(jnp.bfloat16)
        grad_key[:, at] = product(pre_grad, wk_h, (1, 1)).astype(jnp.bfloat16)
        core_copy(1, h).start()

        @pl.when(h >= 2)
        def _():
            relay(1, h - 2)

    lag = 3 + 6 * (top - y)

    @pl.loop(0, heads + 3 + 6 * top)
    def _(step):
        @pl.when(step < heads)
        def _():
            forward(step)

        @pl.when(step >= 3)
        def _():
            @pl.when(step < heads + 3)
            def _():
                relay(0, step - 3)

        @pl.when(step >= lag)
        def _():
            @pl.when(step < lag + heads)
            def _():
                backward(step - lag)

    relay(1, heads - 2)
    relay(1, heads - 1)

    for which in range(2):
        for side in range(2):
            block[side, sent[which], which] = summed[which, side, sent[which]]

        @pl.loop(2, heads)
        def _(h):
            z_copy(which, h).wait_recv()
            block[h % 2, sent[which], which] += rz[which, h, sent[which]]

    for side in range(2):
        block[side, tiles, 1] = jnp.zeros((8, HEAD), jnp.float32)
    low_copy = exchange(block.at[1 - low], rlo, slo, klo, to_low)
    low_copy.start()
    low_copy.wait_recv()
    slim[...] = block[low] + rlo[...]

    def row_copy(k):
        return exchange(slim.at[(y + k) % rows], rrow.at[k, pl.ds(0, 2)], srow.at[k], krow.at[k], to_y(k))

    def gain_copy(k):
        return exchange(slim.at[tiles, pl.ds(0, 1)], rrow.at[k, pl.ds(2, 1)], srowg.at[k], krowg.at[k], to_y(k))

    @pl.loop(1, rows)
    def _(k):
        row_copy(k).start()
        gain_copy(k).start()

    mine[pl.ds(0, 2)] = slim[y]
    mine[pl.ds(2, 1)] = slim[tiles, pl.ds(0, 1)]

    @pl.loop(1, rows)
    def _(k):
        row_copy(k).wait_recv()
        gain_copy(k).wait_recv()
        mine[...] += rrow[k]

    half_copy = exchange(mine, rhi, shi, khi, partner)
    half_copy.start()
    half_copy.wait()
    mine[...] += rhi[...]

    def gather_copy(k, at):
        return exchange(mine.at[pl.ds(0, 2)], full.at[at], sg.at[k], kg.at[k], to_y(k))

    @pl.loop(1, rows)
    def _(k):
        gather_copy(k, y).start()

    out_wq[y] = mine[0]
    out_wk[y] = mine[1]
    first_core = jnp.where(core == 0, 1.0, 0.0).astype(jnp.float32)
    gains = mine[2]
    out_gain[...] = first_core * gains[:1, : HEAD // 2] + (1.0 - first_core) * gains[:1, HEAD // 2 :]

    @pl.loop(1, rows)
    def _(k):
        at = (y + rows - k) % rows
        gather_copy(k, at).wait_recv()
        out_wq[at] = full[at, 0]
        out_wk[at] = full[at, 1]

    low_copy.wait_send()

    @pl.loop(1, rows)
    def _(k):
        row_copy(k).wait_send()
        gain_copy(k).wait_send()
        gather_copy(k, y).wait_send()

    for which in range(2):
        @pl.loop(0, heads)
        def _(h):
            core_copy(which, h).wait_send()

            @pl.when(h >= 2)
            def _():
                z_copy(which, h).wait_send()

    @pl.loop(0, heads)
    def _(h):
        across(h).wait_send()
        across_adj(h).wait_send()

        for p in range(PIECES):
            @pl.when(y != top)
            def _():
                upward(h, p).wait_send()

            @pl.when(y != 0)
            def _():
                downward(h, p).wait_send()


def attention(query, key, value, cotangent, wq, wk, gain, depth, rows):
    heads = wq.shape[0] // HEAD
    tokens, width = query.shape
    tiles = HEAD // 16
    states = pltpu.VMEM((heads, HEAD, HEAD), jnp.float32)
    dma, pieces = pltpu.SemaphoreType.DMA((heads,)), pltpu.SemaphoreType.DMA((heads, PIECES))
    one, each = pltpu.SemaphoreType.DMA, pltpu.SemaphoreType.DMA((rows,))

    def f32(*shape):
        return pltpu.VMEM(shape + (8, HEAD), jnp.float32)

    vmem = pl.BlockSpec(memory_space=pltpu.VMEM)
    grads = jax.ShapeDtypeStruct((tokens, width), jnp.bfloat16)
    return pl.pallas_call(
        functools.partial(attention_kernel, depth, rows),
        out_shape=(grads, grads, grads,
                   jax.ShapeDtypeStruct((tiles, 8, HEAD), jnp.float32),
                   jax.ShapeDtypeStruct((tiles, 8, HEAD), jnp.float32),
                   jax.ShapeDtypeStruct((1, HEAD // 2), jnp.float32)),
        in_specs=[vmem] * 7,
        out_specs=(vmem,) * 6,
        scratch_shapes=[states] * 8
        + [pltpu.VMEM((heads, tokens, HEAD), jnp.bfloat16), pltpu.VMEM((heads, tokens, HEAD), jnp.float32)]
        + [pltpu.VMEM((heads, tokens, HEAD), jnp.float32)] * 2
        + [f32(2, 2, heads, tiles + 1), f32(2, heads, tiles + 1), f32(2, heads, tiles + 1), f32(2, heads, tiles + 1)]
        + [f32(2, tiles + 1, 2), f32(tiles + 1, 2), f32(tiles + 1, 2), f32(rows, 3), f32(3), f32(3), f32(rows, 2)]
        + [dma, dma, pieces, pieces] * 2
        + [pltpu.SemaphoreType.DMA((2, heads))] * 4
        + [one, one, each, each, each, each, one, one, each, each],
        compiler_params=pltpu.CompilerParams(collective_id=0, has_side_effects=True),
        name="attention",
    )(query, key, value, cotangent, wq, wk, gain)


def per_device(depth, rows, query_in, key_in, value_in, grad_out, w_query, w_key, norm_gain):
    width_all = query_in.shape[2]
    grad_query, grad_key, grad_value, total_wq, total_wk, total_gain = attention(
        query_in[0], key_in[0], value_in[0], grad_out[0], w_query, w_key, norm_gain.reshape(1, width_all), depth, rows)
    own = HEAD // 2
    return (
        grad_query[None],
        grad_key[None],
        grad_value[None],
        total_wq.reshape(own, HEAD),
        total_wk.reshape(own, HEAD),
        total_gain.reshape(own),
    )


def solution(mesh):
    tokens = P("dp", "seq", None)
    body = functools.partial(per_device, mesh.shape["dp"] // 4, mesh.shape["seq"] // 2)
    return jax.shard_map(
        body,
        mesh=mesh,
        in_specs=(tokens, tokens, tokens, tokens, P(), P(), P()),
        out_specs=(tokens, tokens, tokens, P("dp", None), P("dp", None), P("dp")),
        check_vma=False,
    )
```
